32 devices in a mesh: grp: 2 (over y), dev: 16 (over z, x, core).
Axes of the slice: x: 2, y: 2, z: 4, core: 2. Of those that a mesh axis runs over, the one named last changes fastest.
Arguments:
- spectra: float32 [256, 2, 2, 4096], P(('grp', 'dev')), may hold values from -100 to 100
- source_pick: int32 [32], P(('grp', 'dev')), may hold values from 0 to 7
- pair_remote: int32 [2, 16, 2, 2], P('grp', 'dev'), may hold values from 0 to 7
- pair_local: int32 [2, 16, 2, 2], P('grp', 'dev'), may hold values from 0 to 7
- pair_count: int32 [2, 16, 2], P('grp', 'dev'), may hold values from 0 to 2, as said below
Outputs:
- group_corr: float32 [256, 16, 512], P(('grp', 'dev'))
- cross_corr: float32 [2, 16, 2, 2, 512], P('grp', 'dev')
The draws below stay inside these ranges and needn't reach their ends.
Inputs may be any that keep to these rules, and one draw needn't show every extreme that they name: `pair_count`: A block has no pairs with its own group and at most 2 with any other; in every group some block has exactly 2 with some other group.
All inputs are finite; a program needn't handle non-finite values.
Results may differ from the reference program's by a relative error of at most 0.0075.
Values may be sent and summed in bfloat16 or wider, within the bound.
A program may use at most 64 MiB of HBM per device.

```python
import math
import jax
import jax.numpy as jnp
from jax import lax

F = 4096
LAGS = 512
LAG_BLK = 128
BAND = 64
SEG = 2
CH_DEV = 8
XCAP = 2
BLOCKS = 32
CHANNELS = 256
N_GRP = 2
N_DEV = 16


def draw_spectra(key, part):
    noise_key, scale_key = jax.random.split(key, 2)
    bands = F // BAND
    noise_base = jnp.clip(jax.random.normal(noise_key, (CHANNELS, SEG, 2, F), jnp.float32), -6.0, 6.0)
    log_scale = jax.random.uniform(scale_key, (CHANNELS, SEG, 1, bands), jnp.float32, 0.0, math.log(10.0))
    band_scale = jnp.repeat(jnp.exp(log_scale), BAND, axis=3)
    return noise_base * band_scale


def draw_pair_count(key, part):
    base_key, block_key, offset_key = jax.random.split(key, 3)
    counts = jax.random.randint(base_key, (N_GRP, N_DEV, N_GRP), 0, XCAP + 1)
    full_block = jax.random.randint(block_key, (N_GRP, 1, 1), 0, N_DEV)
    offset = jax.random.randint(offset_key, (N_GRP, 1, 1), 1, N_GRP)
    own_group = jnp.arange(N_GRP, dtype=jnp.int32)[:, None, None]
    block_index = jnp.arange(N_DEV, dtype=jnp.int32)[None, :, None]
    other_group = jnp.arange(N_GRP, dtype=jnp.int32)[None, None, :]
    full_group = (own_group + offset) % N_GRP
    forced = (block_index == full_block) & (other_group == full_group)
    counts = jnp.where(forced, XCAP, counts)
    return jnp.where(other_group == own_group, 0, counts).astype(jnp.int32)


def touch_ends(drawn, stream_key, smallest, largest):
    longest = drawn.shape.index(max(drawn.shape))
    spots = []
    for shift in (0, 1):
        where = [jax.random.randint(jax.random.fold_in(stream_key, axis), (), 0, length) for axis, length in enumerate(drawn.shape)]
        where[longest] = (where[longest] + shift) % drawn.shape[longest]
        spots.append(tuple(where))
    return drawn.at[spots[0]].set(smallest).at[spots[1]].set(largest)


def setup_inputs(seed: int = 0) -> dict:
    arg_keys = jax.random.split(jax.random.key(seed), 6)
    spectra = draw_spectra(jax.random.fold_in(arg_keys[5], 71), 0)
    source_pick = touch_ends(jax.random.randint(arg_keys[1], (BLOCKS,), 0, CH_DEV), jax.random.fold_in(arg_keys[1], 1), 0, CH_DEV - 1).astype(jnp.int32)
    pair_remote = touch_ends(jax.random.randint(arg_keys[2], (N_GRP, N_DEV, N_GRP, XCAP), 0, CH_DEV), jax.random.fold_in(arg_keys[2], 1), 0, CH_DEV - 1).astype(jnp.int32)
    pair_local = touch_ends(jax.random.randint(arg_keys[3], (N_GRP, N_DEV, N_GRP, XCAP), 0, CH_DEV), jax.random.fold_in(arg_keys[3], 1), 0, CH_DEV - 1).astype(jnp.int32)
    pair_count = draw_pair_count(jax.random.fold_in(arg_keys[5], 71), 0)
    return {"spectra": spectra, "source_pick": source_pick, "pair_remote": pair_remote, "pair_local": pair_local, "pair_count": pair_count}


def whiten(spectra):
    magnitude = jnp.sqrt(spectra[:, :, 0] * spectra[:, :, 0] + spectra[:, :, 1] * spectra[:, :, 1])
    rows_here, segments, bins = magnitude.shape
    band_mean = lax.optimization_barrier(jnp.mean(magnitude.reshape(rows_here, segments, bins // BAND, BAND), axis=3)) + 1e-05
    divisor = jnp.repeat(band_mean, BAND, axis=2)
    return (spectra / divisor[:, :, None, :]).astype(jnp.bfloat16)

def lag_tables():
    frequency = jnp.arange(F, dtype=jnp.int32)
    lag_index = jnp.arange(LAG_BLK, dtype=jnp.int32)
    phase_index = frequency[:, None] * lag_index[None, :] % (2 * F)
    angles = phase_index.astype(jnp.float32) * (math.pi / F)
    return (jnp.cos(angles).astype(jnp.bfloat16), (-jnp.sin(angles)).astype(jnp.bfloat16))

def lag_turn(block_index):
    frequency = jnp.arange(F, dtype=jnp.int32)
    phase_index = frequency * (LAG_BLK * block_index - LAGS // 2) % (2 * F)
    angles = phase_index.astype(jnp.float32) * (math.pi / F)
    return (jnp.cos(angles), jnp.sin(angles))

def cross_to_lags(cross_real, cross_imag, tables):
    cos_table, sin_table = tables
    lag_blocks = []
    for block_index in range(LAGS // LAG_BLK):
        turn_cos, turn_sin = lag_turn(block_index)
        rot_real = (cross_real * turn_cos - cross_imag * turn_sin).astype(jnp.bfloat16)
        rot_imag = (cross_real * turn_sin + cross_imag * turn_cos).astype(jnp.bfloat16)
        lag_blocks.append(jnp.dot(rot_real, cos_table, preferred_element_type=jnp.float32) + jnp.dot(rot_imag, sin_table, preferred_element_type=jnp.float32))
    return jnp.concatenate(lag_blocks, axis=1) * F ** (-0.5)

def outer_cross(left_rows, right_rows):
    left_float = left_rows.astype(jnp.float32)
    right_float = right_rows.astype(jnp.float32)
    segments = left_rows.shape[1]
    cross_real = jnp.zeros((left_rows.shape[0], right_rows.shape[0], F), jnp.float32)
    cross_imag = jnp.zeros((left_rows.shape[0], right_rows.shape[0], F), jnp.float32)
    for segment in range(segments):
        left_real = left_float[:, segment, 0][:, None]
        left_imag = left_float[:, segment, 1][:, None]
        right_real = right_float[:, segment, 0][None]
        right_imag = right_float[:, segment, 1][None]
        cross_real = cross_real + (left_real * right_real + left_imag * right_imag)
        cross_imag = cross_imag + (left_imag * right_real - left_real * right_imag)
    inverse = 1.0 / segments
    return ((cross_real * inverse).reshape(-1, F), (cross_imag * inverse).reshape(-1, F))

def pair_cross(left_rows, right_rows):
    left_float = left_rows.astype(jnp.float32)
    right_float = right_rows.astype(jnp.float32)
    segments = left_rows.shape[1]
    cross_real = jnp.zeros((left_rows.shape[0], F), jnp.float32)
    cross_imag = jnp.zeros((left_rows.shape[0], F), jnp.float32)
    for segment in range(segments):
        left_real = left_float[:, segment, 0]
        left_imag = left_float[:, segment, 1]
        right_real = right_float[:, segment, 0]
        right_imag = right_float[:, segment, 1]
        cross_real = cross_real + (left_real * right_real + left_imag * right_imag)
        cross_imag = cross_imag + (left_imag * right_real - left_real * right_imag)
    inverse = 1.0 / segments
    return (cross_real * inverse, cross_imag * inverse)

def outer_lags(left_rows, right_rows, tables):
    cross_real, cross_imag = outer_cross(left_rows, right_rows)
    return cross_to_lags(cross_real, cross_imag, tables).reshape(left_rows.shape[0], right_rows.shape[0], LAGS)

def reference(spectra, source_pick, pair_remote, pair_local, pair_count):
    white = whiten(spectra)
    tables = lag_tables()
    blocks = white.reshape(N_GRP, N_DEV, CH_DEV, SEG, 2, F)
    sources = blocks[jnp.arange(N_GRP)[:, None], jnp.arange(N_DEV)[None, :], source_pick.reshape(N_GRP, N_DEV)]
    group_ids = jnp.repeat(jnp.arange(N_GRP, dtype=jnp.int32), N_DEV)
    dev_ids = jnp.tile(jnp.arange(N_DEV, dtype=jnp.int32), N_GRP)

    def one_block(entry):
        group_id, dev_id = entry
        return outer_lags(blocks[group_id, dev_id], sources[group_id], tables)
    group_corr = lax.map(one_block, (group_ids, dev_ids)).reshape(CHANNELS, N_DEV, LAGS)

    def one_receiver(entry):
        group_id, dev_id, remote_ids, local_ids, counts = entry
        column = blocks[:, dev_id]
        remote_rows = column[jnp.arange(N_GRP)[:, None], remote_ids]
        local_rows = blocks[group_id, dev_id][local_ids]
        cross_real, cross_imag = pair_cross(local_rows.reshape(-1, SEG, 2, F), remote_rows.reshape(-1, SEG, 2, F))
        lags_out = cross_to_lags(cross_real, cross_imag, tables).reshape(N_GRP, XCAP, LAGS)
        valid_mask = (jnp.arange(XCAP)[None, :] < counts[:, None]).astype(jnp.float32)
        return lags_out * valid_mask[:, :, None]
    cross_corr = lax.map(one_receiver, (group_ids, dev_ids, pair_remote.reshape(BLOCKS, N_GRP, XCAP), pair_local.reshape(BLOCKS, N_GRP, XCAP), pair_count.reshape(BLOCKS, N_GRP)))
    return (group_corr, cross_corr.reshape(N_GRP, N_DEV, N_GRP, XCAP, LAGS))
```

```python
import functools

import jax
import jax.numpy as jnp
import numpy as np
from jax import lax
from jax.experimental import pallas as pl
from jax.experimental.pallas import tpu as pltpu
from jax.sharding import PartitionSpec as P

MESH = pl.DeviceIdType.MESH
F = 4096
LAGS = 512
HALF = LAGS // 2
BAND = 64
CHUNKS = 4
WIDE = F // CHUNKS
LANES = 128
INNER = 256
BLK = F // INNER
SCALE = 0.5 * F ** (-0.5)
f32, bf16 = jnp.float32, jnp.bfloat16


def lag_tables():
    lag = np.arange(HALF)
    lag[0] = HALF
    angle = np.pi * ((np.arange(INNER)[:, None] * lag[None, :]) % (2 * F)) / F
    table = np.concatenate([np.cos(angle), np.sin(angle)], axis=1)
    turn = np.pi * ((np.arange(BLK)[:, None] * np.arange(LANES)[None, :]) % (2 * BLK)) / BLK
    turn = SCALE * np.stack([np.cos(turn), np.sin(turn)])
    return table.astype(jnp.bfloat16), np.repeat(turn[:, :, None, :], 8, axis=2).astype(np.float32)


def kernel(
    groups, n_dev, slots, channels,
    pick_ref, remote_hbm, local_hbm, count_hbm, x_hbm, table_hbm, turn_hbm,
    acc, cross_out,
    raw, white, mag, gathered, row_scratch, src_f32, x, y, table, turn, pr, pi,
    req_out, req_in, rows_out, rows_in, remote_ref, local_ref, count_ref,
    load_sem, small_sem, send_sem, recv_sem, req_send, req_recv, row_send, row_recv,
):
    g = lax.axis_index("grp")
    d = lax.axis_index("dev")
    rows = n_dev // 4
    r, c, k = d // 4, (d // 2) % 2, d % 2
    flip_k = r * 4 + c * 2 + (1 - k)
    across = [r * 4 + (1 - c) * 2 + k, r * 4 + (1 - c) * 2 + (1 - k)]

    def row_of(t):
        if rows == 4:
            return [r, r + 1 - 2 * (r % 2), 2 - r // 2, 3 - 3 * (r // 2)][t]
        return lax.rem(r + t, rows)

    def group_of(t):
        return lax.rem(g + t, groups)

    loads = [
        pltpu.make_async_copy(x_hbm.at[:, sp // 2, sp % 2, :], raw.at[sp], load_sem.at[sp]) for sp in range(4)
    ]
    remote_load = pltpu.make_async_copy(remote_hbm, remote_ref, small_sem.at[0])
    local_load = pltpu.make_async_copy(local_hbm, local_ref, small_sem.at[1])
    count_load = pltpu.make_async_copy(count_hbm, count_ref, small_sem.at[2])
    table_load = pltpu.make_async_copy(table_hbm, table, small_sem.at[3])
    turn_load = pltpu.make_async_copy(turn_hbm, turn, small_sem.at[4])
    for copy in loads + [remote_load, local_load, count_load, table_load, turn_load]:
        copy.start()

    barrier = pltpu.get_barrier_semaphore()
    for t in range(1, rows):
        pl.semaphore_signal(barrier, inc=1, device_id=(g, row_of(t) * 4 + c * 2 + k), device_id_type=MESH)
    for target in across + [flip_k]:
        pl.semaphore_signal(barrier, inc=1, device_id=(g, target), device_id_type=MESH)
    for t in range(1, groups):
        pl.semaphore_signal(barrier, inc=1, device_id=(group_of(t), d), device_id_type=MESH)

    started = []

    def remote(src, dst, send, recv, target):
        return pltpu.make_async_remote_copy(
            src_ref=src, dst_ref=dst, send_sem=send, recv_sem=recv, device_id=target, device_id_type=MESH
        )

    lane_i = lax.broadcasted_iota(jnp.int32, (LANES, LANES), 0)
    lane_j = lax.broadcasted_iota(jnp.int32, (LANES, LANES), 1)
    averaging = jnp.where(lane_i // BAND == lane_j // BAND, 1.0 / BAND, 0.0).astype(bf16)
    tiles = F // LANES

    def whiten():
        for s in range(2):
            for l in range(tiles):
                cols = slice(l * LANES, (l + 1) * LANES)
                re, im = raw[2 * s, :, cols], raw[2 * s + 1, :, cols]
                mag[(s * tiles + l) * channels:(s * tiles + l + 1) * channels, :] = jnp.sqrt(re * re + im * im)
        value = mag[...]
        high = value.astype(bf16)
        rest = value - high.astype(f32)
        mid = rest.astype(bf16)
        low = (rest - mid.astype(f32)).astype(bf16)
        mean = (
            jnp.dot(high, averaging, preferred_element_type=f32)
            + jnp.dot(mid, averaging, preferred_element_type=f32)
            + jnp.dot(low, averaging, preferred_element_type=f32)
        )
        mag[...] = 1.0 / (mean + 1e-05)
        for s in range(2):
            for l in range(tiles):
                cols = slice(l * LANES, (l + 1) * LANES)
                inverse = mag[(s * tiles + l) * channels:(s * tiles + l + 1) * channels, :]
                for p in range(2):
                    scaled = raw[2 * s + p, :, cols] * inverse
                    white[2 * s + p, :, cols] = scaled.astype(bf16).astype(f32)

    def pick_row(channel):
        for sp in range(4):
            for i in range(CHUNKS):
                row_scratch[sp * CHUNKS + i:sp * CHUNKS + i + 1, :] = white[
                    sp, pl.ds(channel, 1), i * WIDE:(i + 1) * WIDE
                ]

    n_sent = [0]

    def forward(j, target):
        copy = remote(gathered.at[j], gathered.at[j], send_sem.at[n_sent[0]], recv_sem.at[j], (g, target))
        n_sent[0] += 1
        copy.start()
        started.append(copy)

    def arrived(j):
        remote(gathered.at[j], gathered.at[j], send_sem.at[0], recv_sem.at[j], (g, flip_k)).wait_recv()

    def transform(base, zero):
        y[...] = jnp.dot(x[...], table[...], preferred_element_type=f32)
        for h in range(2):
            p = [jnp.zeros((8, LANES), f32) for _ in range(2)]
            q = [jnp.zeros((8, LANES), f32) for _ in range(2)]
            for b in range(BLK):
                cos, sin = turn[0, b], turn[1, b]
                real = slice(b * 16 + h * 8, b * 16 + h * 8 + 8)
                imag = slice(HALF + b * 16 + h * 8, HALF + b * 16 + h * 8 + 8)
                for u in range(2):
                    on_cos = slice(u * LANES, (u + 1) * LANES)
                    on_sin = slice(HALF + u * LANES, HALF + (u + 1) * LANES)
                    p[u] = p[u] + (cos * y[real, on_cos] - sin * y[real, on_sin])
                    q[u] = q[u] + (cos * y[imag, on_sin] + sin * y[imag, on_cos])
            lane = lax.broadcasted_iota(jnp.int32, (8, LANES), 1)
            back = lax.rem(LANES - lane, LANES)
            turned = [jnp.take_along_axis(p[u] + q[u], back, axis=1) for u in range(2)]
            out = [
                jnp.where(lane == 0, turned[0], turned[1]),
                jnp.where(lane == 0, turned[1], turned[0]),
                jnp.where(lane == 0, zero[h] * SCALE, p[0] - q[0]),
                p[1] - q[1],
            ]
            for n in range(4):
                acc[pl.ds(base + h * 8, 8), n * LANES:(n + 1) * LANES] = out[n]

    def batch(first):
        for half in range(2):
            src_f32[half] = gathered[first + half].astype(f32)
        total = [jnp.zeros((channels, LANES), f32) for _ in range(2)]
        for l in range(tiles):
            i, lanes = l // 8, slice(l % 8 * LANES, (l % 8 + 1) * LANES)
            w = [white[sp, :, l * LANES:(l + 1) * LANES] for sp in range(4)]
            real, imag = [], []
            for half in range(2):
                v = [
                    jnp.broadcast_to(
                        src_f32[half, sp * CHUNKS + i:sp * CHUNKS + i + 1, lanes], (channels, LANES)
                    )
                    for sp in range(4)
                ]
                real.append(w[0] * v[0] + w[1] * v[1] + w[2] * v[2] + w[3] * v[3])
                imag.append(w[1] * v[0] - w[0] * v[1] + w[3] * v[2] - w[2] * v[3])
                total[half] = total[half] + real[-1]
            b, cols = l // 2, slice(l % 2 * LANES, (l % 2 + 1) * LANES)
            x[b * 16:(b + 1) * 16, cols] = jnp.concatenate(real, axis=0).astype(bf16)
            x[HALF + b * 16:HALF + (b + 1) * 16, cols] = jnp.concatenate(imag, axis=0).astype(bf16)
        transform(
            pl.multiple_of(first * channels, 2 * channels), [jnp.sum(t, axis=1, keepdims=True) for t in total]
        )

    for copy in loads:
        copy.wait()
    whiten()
    pick_row(pick_ref[0])
    gathered[d] = row_scratch[...].astype(bf16)
    remote_load.wait()
    for t in range(1, groups):
        h = group_of(t)
        for slot in range(slots):
            req_out[t, slot:slot + 1, :] = jnp.full((1, LANES), remote_ref[0, 0, h, slot], jnp.int32)

    pl.semaphore_wait(barrier, rows + 2 + groups - 1)
    for t in range(rows - 1, 0, -1):
        forward(d, row_of(t) * 4 + c * 2 + k)
    for target in across + [flip_k]:
        forward(d, target)
    for t in range(1, groups):
        copy = remote(req_out.at[t], req_in.at[g], req_send.at[t], req_recv.at[g], (group_of(t), d))
        copy.start()
        started.append(copy)

    table_load.wait()
    turn_load.wait()
    arrived(flip_k)
    batch(r * 4 + c * 2)

    channel_id = lax.broadcasted_iota(jnp.int32, (channels, LANES), 0)
    for t in range(1, groups):
        h = group_of(t)
        remote(req_out.at[t], req_in.at[h], req_send.at[t], req_recv.at[h], (h, d)).wait_recv()
        asked = req_in[h]
        for slot in range(slots):
            chosen = channel_id == jnp.broadcast_to(asked[slot:slot + 1, :], (channels, LANES))
            chosen = jnp.concatenate([chosen] * (WIDE // LANES), axis=1)
            for sp in range(4):
                for q in range(CHUNKS):
                    part = jnp.where(chosen, white[sp, :, q * WIDE:(q + 1) * WIDE], 0.0)
                    row_scratch[sp * CHUNKS + q:sp * CHUNKS + q + 1, :] = jnp.sum(part, axis=0, keepdims=True)
            rows_out[t, slot * 16:(slot + 1) * 16, :] = row_scratch[...].astype(bf16)
        copy = remote(rows_out.at[t], rows_in.at[g], row_send.at[t], row_recv.at[g], (h, d))
        copy.start()
        started.append(copy)

    for t in range(1, rows):
        j = row_of(t) * 4 + c * 2 + k
        arrived(j)
        for target in across + [flip_k]:
            forward(j, target)

    def chips(first_t, column):
        @pl.loop(first_t, rows)
        def _(t):
            if rows == 4:
                row = jnp.where(t == 0, r, jnp.where(t == 1, row_of(1), jnp.where(t == 2, row_of(2), row_of(3))))
            else:
                row = lax.rem(r + t, rows)
            first = row * 4 + column * 2
            if first_t == 0:
                arrived(first)
                arrived(first + 1)
            else:
                arrived(first + (1 - k))
            batch(first)

    chips(1, c)

    local_load.wait()
    count_load.wait()
    cross_out[0, 0, g] = jnp.zeros((slots, LAGS), f32)
    pairs = (groups - 1) * slots
    for base in range(0, pairs, 16):
        pr[...] = jnp.zeros_like(pr)
        pi[...] = jnp.zeros_like(pi)
        for n in range(base, min(base + 16, pairs)):
            t, slot = n // slots + 1, n % slots
            h = group_of(t)
            if slot == 0:
                remote(rows_out.at[t], rows_in.at[h], row_send.at[t], row_recv.at[h], (h, d)).wait_recv()
            pick_row(local_ref[0, 0, h, slot])
            there = rows_in[h, slot * 16:(slot + 1) * 16, :].astype(f32)
            here = row_scratch[...]
            w = [here[sp * CHUNKS:(sp + 1) * CHUNKS] for sp in range(4)]
            v = [there[sp * CHUNKS:(sp + 1) * CHUNKS] for sp in range(4)]
            real = w[0] * v[0] + w[1] * v[1] + w[2] * v[2] + w[3] * v[3]
            imag = w[1] * v[0] - w[0] * v[1] + w[3] * v[2] - w[2] * v[3]
            for q in range(CHUNKS):
                pr[n - base:n - base + 1, q * WIDE:(q + 1) * WIDE] = real[q:q + 1]
                pi[n - base:n - base + 1, q * WIDE:(q + 1) * WIDE] = imag[q:q + 1]
        for b in range(BLK):
            x[b * 16:(b + 1) * 16, :] = pr[:, b * INNER:(b + 1) * INNER].astype(bf16)
            x[HALF + b * 16:HALF + (b + 1) * 16, :] = pi[:, b * INNER:(b + 1) * INNER].astype(bf16)
        zero = [jnp.sum(pr[h * 8:(h + 1) * 8, :], axis=1, keepdims=True) for h in range(2)]
        transform(n_dev * channels, zero)
        for n in range(base, min(base + 16, pairs)):
            t, slot = n // slots + 1, n % slots
            h = group_of(t)
            row = n_dev * channels + n - base
            keep = jnp.where(slot < count_ref[0, 0, h], 1.0, 0.0)
            cross_out[0, 0, h, slot:slot + 1, :] = acc[row:row + 1, :] * keep

    chips(0, 1 - c)

    for copy in started:
        copy.wait_send()


def store(n_dev, acc, cross_in, group_out, cross_out, sem):
    channels = group_out.shape[0]
    copies = [
        pltpu.make_async_copy(acc.at[0:n_dev, ch, :], group_out.at[ch], sem.at[ch]) for ch in range(channels)
    ] + [pltpu.make_async_copy(cross_in, cross_out, sem.at[channels])]
    for copy in copies:
        copy.start()
    for copy in copies:
        copy.wait()


def solution(mesh):
    groups, n_dev = mesh.shape["grp"], mesh.shape["dev"]
    table, turn = lag_tables()

    def on_device(spectra, source_pick, pair_remote, pair_local, pair_count):
        channels = spectra.shape[0]
        slots = pair_remote.shape[3]
        total = n_dev * channels + 16
        hbm = pl.BlockSpec(memory_space=pltpu.HBM)
        vmem = pl.BlockSpec(memory_space=pltpu.VMEM)
        anywhere = pl.BlockSpec(memory_space=pl.ANY)
        held = [
            pltpu.with_memory_space_constraint(a, pltpu.HBM)
            for a in (pair_remote, pair_local, pair_count, spectra, jnp.asarray(table), jnp.asarray(turn))
        ]
        cross_shape = (1, 1, groups, slots, LAGS)
        sends = 3 * rows_of(n_dev) + rows_of(n_dev) - 1
        acc, cross = pl.pallas_call(
            functools.partial(kernel, groups, n_dev, slots, channels),
            out_shape=(pltpu.VMEM((total, LAGS), f32), pltpu.VMEM(cross_shape, f32)),
            in_specs=[pl.BlockSpec(memory_space=pltpu.SMEM)] + [hbm] * 6,
            out_specs=(vmem, vmem),
            scratch_shapes=[
                pltpu.VMEM((4, channels, F), f32),
                pltpu.VMEM((4, channels, F), f32),
                pltpu.VMEM((2 * F // LANES * channels, LANES), f32),
                pltpu.VMEM((n_dev, 16, WIDE), bf16),
                pltpu.VMEM((16, WIDE), f32),
                pltpu.VMEM((2, 16, WIDE), f32),
                pltpu.VMEM((2 * HALF, INNER), bf16),
                pltpu.VMEM((2 * HALF, 2 * HALF), f32),
                pltpu.VMEM(table.shape, bf16),
                pltpu.VMEM(turn.shape, f32),
                pltpu.VMEM((16, F), f32),
                pltpu.VMEM((16, F), f32),
                pltpu.VMEM((groups, 8, LANES), jnp.int32),
                pltpu.VMEM((groups, 8, LANES), jnp.int32),
                pltpu.VMEM((groups, slots * 16, WIDE), bf16),
                pltpu.VMEM((groups, slots * 16, WIDE), bf16),
                pltpu.SMEM(pair_remote.shape, jnp.int32),
                pltpu.SMEM(pair_local.shape, jnp.int32),
                pltpu.SMEM(pair_count.shape, jnp.int32),
                pltpu.SemaphoreType.DMA((4,)),
                pltpu.SemaphoreType.DMA((5,)),
                pltpu.SemaphoreType.DMA((sends,)),
                pltpu.SemaphoreType.DMA((n_dev,)),
                pltpu.SemaphoreType.DMA((groups,)),
                pltpu.SemaphoreType.DMA((groups,)),
                pltpu.SemaphoreType.DMA((groups,)),
                pltpu.SemaphoreType.DMA((groups,)),
            ],
            compiler_params=pltpu.CompilerParams(
                collective_id=0, has_side_effects=True, vmem_limit_bytes=48 << 20
            ),
        )(source_pick, *held)
        return pl.pallas_call(
            functools.partial(store, n_dev),
            out_shape=(
                jax.ShapeDtypeStruct((channels, n_dev, LAGS), f32),
                jax.ShapeDtypeStruct(cross_shape, f32),
            ),
            in_specs=[anywhere, anywhere],
            out_specs=(anywhere, anywhere),
            scratch_shapes=[pltpu.SemaphoreType.DMA((channels + 1,))],
            compiler_params=pltpu.CompilerParams(vmem_limit_bytes=1 << 20),
        )(acc.reshape(total // channels, channels, LAGS), cross)

    return jax.shard_map(
        on_device,
        mesh=mesh,
        in_specs=(
            P(("grp", "dev"), None, None, None),
            P(("grp", "dev")),
            P("grp", "dev", None, None),
            P("grp", "dev", None, None),
            P("grp", "dev", None),
        ),
        out_specs=(P(("grp", "dev"), None, None), P("grp", "dev", None, None, None)),
        check_vma=False,
    )


def rows_of(n_dev):
    return n_dev // 4
```

```python
import functools

import jax
import jax.numpy as jnp
import numpy as np
from jax import lax
from jax.experimental import pallas as pl
from jax.experimental.pallas import tpu as pltpu
from jax.sharding import PartitionSpec as P

MESH = pl.DeviceIdType.MESH
F = 4096
LAGS = 512
HALF = LAGS // 2
BAND = 64
CHUNKS = 4
DIRECT = 2
WIDE = F // CHUNKS
LANES = 128
INNER = 256
BLK = F // INNER
SCALE = 0.5 * F ** (-0.5)
f32, bf16 = jnp.float32, jnp.bfloat16


def lag_tables():
    lag = np.arange(HALF)
    lag[0] = HALF
    angle = np.pi * ((np.arange(INNER)[:, None] * lag[None, :]) % (2 * F)) / F
    table = np.concatenate([np.cos(angle), np.sin(angle)], axis=1)
    turn = np.pi * ((np.arange(BLK)[:, None] * np.arange(LANES)[None, :]) % (2 * BLK)) / BLK
    turn = SCALE * np.stack([np.cos(turn), np.sin(turn)])
    return table.astype(jnp.bfloat16), np.repeat(turn[:, :, None, :], 8, axis=2).astype(np.float32)


def kernel(
    groups, n_dev, slots, channels,
    pick_ref, remote_hbm, local_hbm, count_hbm, x_hbm, table_hbm, turn_hbm,
    acc, cross_out,
    raw, white, mag, gathered, row_scratch, src_f32, x, y, table, turn, pr, pi,
    req_out, req_in, rows_out, rows_in, remote_ref, local_ref, count_ref,
    load_sem, small_sem, send_sem, recv_sem, req_send, req_recv, row_send, row_recv,
):
    g = lax.axis_index("grp")
    d = lax.axis_index("dev")
    rows = n_dev // 4
    r, c, k = d // 4, (d // 2) % 2, d % 2
    flip_k = r * 4 + c * 2 + (1 - k)
    across = [r * 4 + (1 - c) * 2 + k, r * 4 + (1 - c) * 2 + (1 - k)]

    def row_of(t):
        if rows == 4:
            return [r, r + 1 - 2 * (r % 2), 2 - r // 2, 3 - 3 * (r // 2)][t]
        return lax.rem(r + t, rows)

    def group_of(t):
        return lax.rem(g + t, groups)

    loads = [
        pltpu.make_async_copy(x_hbm.at[:, sp // 2, sp % 2, :], raw.at[sp], load_sem.at[sp]) for sp in range(4)
    ]
    remote_load = pltpu.make_async_copy(remote_hbm, remote_ref, small_sem.at[0])
    local_load = pltpu.make_async_copy(local_hbm, local_ref, small_sem.at[1])
    count_load = pltpu.make_async_copy(count_hbm, count_ref, small_sem.at[2])
    table_load = pltpu.make_async_copy(table_hbm, table, small_sem.at[3])
    turn_load = pltpu.make_async_copy(turn_hbm, turn, small_sem.at[4])
    for copy in loads + [remote_load, local_load, count_load, table_load, turn_load]:
        copy.start()

    barrier = pltpu.get_barrier_semaphore()
    for t in range(1, rows):
        pl.semaphore_signal(barrier, inc=1, device_id=(g, row_of(t) * 4 + c * 2 + k), device_id_type=MESH)
    for target in across + [flip_k]:
        pl.semaphore_signal(barrier, inc=1, device_id=(g, target), device_id_type=MESH)
    for row in range(rows - DIRECT, rows):
        @pl.when(r + c == 0)
        def _():
            pl.semaphore_signal(barrier, inc=1, device_id=(g, row * 4 + across[0] % 4), device_id_type=MESH)
    for t in range(1, groups):
        pl.semaphore_signal(barrier, inc=1, device_id=(group_of(t), d), device_id_type=MESH)

    started = []

    def remote(src, dst, send, recv, target):
        return pltpu.make_async_remote_copy(
            src_ref=src, dst_ref=dst, send_sem=send, recv_sem=recv, device_id=target, device_id_type=MESH
        )

    lane_i = lax.broadcasted_iota(jnp.int32, (LANES, LANES), 0)
    lane_j = lax.broadcasted_iota(jnp.int32, (LANES, LANES), 1)
    averaging = jnp.where(lane_i // BAND == lane_j // BAND, 1.0 / BAND, 0.0).astype(bf16)
    tiles = F // LANES

    def whiten():
        for s in range(2):
            for l in range(tiles):
                cols = slice(l * LANES, (l + 1) * LANES)
                re, im = raw[2 * s, :, cols], raw[2 * s + 1, :, cols]
                mag[(s * tiles + l) * channels:(s * tiles + l + 1) * channels, :] = jnp.sqrt(re * re + im * im)
        value = mag[...]
        high = value.astype(bf16)
        rest = value - high.astype(f32)
        mid = rest.astype(bf16)
        low = (rest - mid.astype(f32)).astype(bf16)
        mean = (
            jnp.dot(high, averaging, preferred_element_type=f32)
            + jnp.dot(mid, averaging, preferred_element_type=f32)
            + jnp.dot(low, averaging, preferred_element_type=f32)
        )
        mag[...] = 1.0 / (mean + 1e-05)
        for s in range(2):
            for l in range(tiles):
                cols = slice(l * LANES, (l + 1) * LANES)
                inverse = mag[(s * tiles + l) * channels:(s * tiles + l + 1) * channels, :]
                for p in range(2):
                    scaled = raw[2 * s + p, :, cols] * inverse
                    white[2 * s + p, :, cols] = scaled.astype(bf16).astype(f32)

    def pick_row(channel):
        for sp in range(4):
            for i in range(CHUNKS):
                row_scratch[sp * CHUNKS + i:sp * CHUNKS + i + 1, :] = white[
                    sp, pl.ds(channel, 1), i * WIDE:(i + 1) * WIDE
                ]

    n_sent = [0]

    def forward(j, target, when=None):
        copy = remote(gathered.at[j], gathered.at[j], send_sem.at[n_sent[0]], recv_sem.at[j], (g, target))
        n_sent[0] += 1
        if when is None:
            copy.start()
        else:
            pl.when(when)(copy.start)
        started.append((when, copy))

    def arrived(j):
        remote(gathered.at[j], gathered.at[j], send_sem.at[0], recv_sem.at[j], (g, flip_k)).wait_recv()

    def transform(base, zero):
        y[...] = jnp.dot(x[...], table[...], preferred_element_type=f32)
        for h in range(2):
            p = [jnp.zeros((8, LANES), f32) for _ in range(2)]
            q = [jnp.zeros((8, LANES), f32) for _ in range(2)]
            for b in range(BLK):
                cos, sin = turn[0, b], turn[1, b]
                real = slice(b * 16 + h * 8, b * 16 + h * 8 + 8)
                imag = slice(HALF + b * 16 + h * 8, HALF + b * 16 + h * 8 + 8)
                for u in range(2):
                    on_cos = slice(u * LANES, (u + 1) * LANES)
                    on_sin = slice(HALF + u * LANES, HALF + (u + 1) * LANES)
                    p[u] = p[u] + (cos * y[real, on_cos] - sin * y[real, on_sin])
                    q[u] = q[u] + (cos * y[imag, on_sin] + sin * y[imag, on_cos])
            lane = lax.broadcasted_iota(jnp.int32, (8, LANES), 1)
            back = lax.rem(LANES - lane, LANES)
            turned = [jnp.take_along_axis(p[u] + q[u], back, axis=1) for u in range(2)]
            out = [
                jnp.where(lane == 0, turned[0], turned[1]),
                jnp.where(lane == 0, turned[1], turned[0]),
                jnp.where(lane == 0, zero[h] * SCALE, p[0] - q[0]),
                p[1] - q[1],
            ]
            for n in range(4):
                acc[pl.ds(base + h * 8, 8), n * LANES:(n + 1) * LANES] = out[n]

    def batch(first):
        for half in range(2):
            src_f32[half] = gathered[first + half].astype(f32)
        total = [jnp.zeros((channels, LANES), f32) for _ in range(2)]
        for l in range(tiles):
            i, lanes = l // 8, slice(l % 8 * LANES, (l % 8 + 1) * LANES)
            w = [white[sp, :, l * LANES:(l + 1) * LANES] for sp in range(4)]
            real, imag = [], []
            for half in range(2):
                v = [
                    jnp.broadcast_to(
                        src_f32[half, sp * CHUNKS + i:sp * CHUNKS + i + 1, lanes], (channels, LANES)
                    )
                    for sp in range(4)
                ]
                real.append(w[0] * v[0] + w[1] * v[1] + w[2] * v[2] + w[3] * v[3])
                imag.append(w[1] * v[0] - w[0] * v[1] + w[3] * v[2] - w[2] * v[3])
                total[half] = total[half] + real[-1]
            b, cols = l // 2, slice(l % 2 * LANES, (l % 2 + 1) * LANES)
            x[b * 16:(b + 1) * 16, cols] = jnp.concatenate(real, axis=0).astype(bf16)
            x[HALF + b * 16:HALF + (b + 1) * 16, cols] = jnp.concatenate(imag, axis=0).astype(bf16)
        transform(
            pl.multiple_of(first * channels, 2 * channels), [jnp.sum(t, axis=1, keepdims=True) for t in total]
        )

    for copy in loads:
        copy.wait()
    whiten()
    pick_row(pick_ref[0])
    gathered[d] = row_scratch[...].astype(bf16)
    remote_load.wait()
    for t in range(1, groups):
        h = group_of(t)
        for slot in range(slots):
            req_out[t, slot:slot + 1, :] = jnp.full((1, LANES), remote_ref[0, 0, h, slot], jnp.int32)

    pl.semaphore_wait(barrier, rows + 2 + groups - 1 + (r + DIRECT) // rows * c)
    straight = (r >= rows - DIRECT) & (c == 1)
    forward(d, across[0] % 4, straight)
    for t in range(rows - 1, 0, -1):
        forward(d, row_of(t) * 4 + c * 2 + k)
    for target in across + [flip_k]:
        forward(d, target)
    for t in range(1, groups):
        copy = remote(req_out.at[t], req_in.at[g], req_send.at[t], req_recv.at[g], (group_of(t), d))
        copy.start()
        started.append((None, copy))

    table_load.wait()
    turn_load.wait()
    arrived(flip_k)
    batch(r * 4 + c * 2)

    channel_id = lax.broadcasted_iota(jnp.int32, (channels, LANES), 0)
    for t in range(1, groups):
        h = group_of(t)
        remote(req_out.at[t], req_in.at[h], req_send.at[t], req_recv.at[h], (h, d)).wait_recv()
        asked = req_in[h]
        for slot in range(slots):
            chosen = channel_id == jnp.broadcast_to(asked[slot:slot + 1, :], (channels, LANES))
            chosen = jnp.concatenate([chosen] * (WIDE // LANES), axis=1)
            for sp in range(4):
                for q in range(CHUNKS):
                    part = jnp.where(chosen, white[sp, :, q * WIDE:(q + 1) * WIDE], 0.0)
                    row_scratch[sp * CHUNKS + q:sp * CHUNKS + q + 1, :] = jnp.sum(part, axis=0, keepdims=True)
            rows_out[t, slot * 16:(slot + 1) * 16, :] = row_scratch[...].astype(bf16)
        copy = remote(rows_out.at[t], rows_in.at[g], row_send.at[t], row_recv.at[g], (h, d))
        copy.start()
        started.append((None, copy))

    for t in range(1, rows):
        j = row_of(t) * 4 + c * 2 + k
        arrived(j)
        for target in across:
            forward(j, target, (r > 0) | (c == 0) if t >= rows - DIRECT else None)
        forward(j, flip_k)

    def chips(first_t, end_t, column):
        @pl.loop(first_t, end_t)
        def _(t):
            if rows == 4:
                row = jnp.where(t == 0, r, jnp.where(t == 1, row_of(1), jnp.where(t == 2, row_of(2), row_of(3))))
            else:
                row = lax.rem(r + t, rows)
            first = row * 4 + column * 2
            if column is not c:
                arrived(first + (1 - k))

                @pl.when(jnp.logical_or(r + c > 0, row < rows - DIRECT))
                def _():
                    arrived(first + k)
            else:
                arrived(first + (1 - k))
            batch(first)

    other = 1 - c
    chips(0, 1, other)
    chips(1, 2, c)
    for row in range(rows - DIRECT, rows):
        j = row * 4 + across[0] % 4
        pl.when(r + c == 0)(functools.partial(arrived, j))
        forward(j, flip_k, r + c == 0)

    chips(2, rows, c)

    local_load.wait()
    count_load.wait()
    cross_out[0, 0, g] = jnp.zeros((slots, LAGS), f32)
    pairs = (groups - 1) * slots
    for base in range(0, pairs, 16):
        pr[...] = jnp.zeros_like(pr)
        pi[...] = jnp.zeros_like(pi)
        for n in range(base, min(base + 16, pairs)):
            t, slot = n // slots + 1, n % slots
            h = group_of(t)
            if slot == 0:
                remote(rows_out.at[t], rows_in.at[h], row_send.at[t], row_recv.at[h], (h, d)).wait_recv()
            pick_row(local_ref[0, 0, h, slot])
            there = rows_in[h, slot * 16:(slot + 1) * 16, :].astype(f32)
            here = row_scratch[...]
            w = [here[sp * CHUNKS:(sp + 1) * CHUNKS] for sp in range(4)]
            v = [there[sp * CHUNKS:(sp + 1) * CHUNKS] for sp in range(4)]
            real = w[0] * v[0] + w[1] * v[1] + w[2] * v[2] + w[3] * v[3]
            imag = w[1] * v[0] - w[0] * v[1] + w[3] * v[2] - w[2] * v[3]
            for q in range(CHUNKS):
                pr[n - base:n - base + 1, q * WIDE:(q + 1) * WIDE] = real[q:q + 1]
                pi[n - base:n - base + 1, q * WIDE:(q + 1) * WIDE] = imag[q:q + 1]
        for b in range(BLK):
            x[b * 16:(b + 1) * 16, :] = pr[:, b * INNER:(b + 1) * INNER].astype(bf16)
            x[HALF + b * 16:HALF + (b + 1) * 16, :] = pi[:, b * INNER:(b + 1) * INNER].astype(bf16)
        zero = [jnp.sum(pr[h * 8:(h + 1) * 8, :], axis=1, keepdims=True) for h in range(2)]
        transform(n_dev * channels, zero)
        for n in range(base, min(base + 16, pairs)):
            t, slot = n // slots + 1, n % slots
            h = group_of(t)
            row = n_dev * channels + n - base
            keep = jnp.where(slot < count_ref[0, 0, h], 1.0, 0.0)
            cross_out[0, 0, h, slot:slot + 1, :] = acc[row:row + 1, :] * keep

    chips(1, rows, other)

    for when, copy in started:
        if when is None:
            copy.wait_send()
        else:
            pl.when(when)(copy.wait_send)


def store(n_dev, acc, cross_in, group_out, cross_out, sem):
    channels = group_out.shape[0]
    copies = [
        pltpu.make_async_copy(acc.at[0:n_dev, ch, :], group_out.at[ch], sem.at[ch]) for ch in range(channels)
    ] + [pltpu.make_async_copy(cross_in, cross_out, sem.at[channels])]
    for copy in copies:
        copy.start()
    for copy in copies:
        copy.wait()


def solution(mesh):
    groups, n_dev = mesh.shape["grp"], mesh.shape["dev"]
    table, turn = lag_tables()

    def on_device(spectra, source_pick, pair_remote, pair_local, pair_count):
        channels = spectra.shape[0]
        slots = pair_remote.shape[3]
        total = n_dev * channels + 16
        hbm = pl.BlockSpec(memory_space=pltpu.HBM)
        vmem = pl.BlockSpec(memory_space=pltpu.VMEM)
        anywhere = pl.BlockSpec(memory_space=pl.ANY)
        held = [
            pltpu.with_memory_space_constraint(a, pltpu.HBM)
            for a in (pair_remote, pair_local, pair_count, spectra, jnp.asarray(table), jnp.asarray(turn))
        ]
        cross_shape = (1, 1, groups, slots, LAGS)
        sends = DIRECT + 2 + 3 * rows_of(n_dev) + rows_of(n_dev) - 1
        acc, cross = pl.pallas_call(
            functools.partial(kernel, groups, n_dev, slots, channels),
            out_shape=(pltpu.VMEM((total, LAGS), f32), pltpu.VMEM(cross_shape, f32)),
            in_specs=[pl.BlockSpec(memory_space=pltpu.SMEM)] + [hbm] * 6,
            out_specs=(vmem, vmem),
            scratch_shapes=[
                pltpu.VMEM((4, channels, F), f32),
                pltpu.VMEM((4, channels, F), f32),
                pltpu.VMEM((2 * F // LANES * channels, LANES), f32),
                pltpu.VMEM((n_dev, 16, WIDE), bf16),
                pltpu.VMEM((16, WIDE), f32),
                pltpu.VMEM((2, 16, WIDE), f32),
                pltpu.VMEM((2 * HALF, INNER), bf16),
                pltpu.VMEM((2 * HALF, 2 * HALF), f32),
                pltpu.VMEM(table.shape, bf16),
                pltpu.VMEM(turn.shape, f32),
                pltpu.VMEM((16, F), f32),
                pltpu.VMEM((16, F), f32),
                pltpu.VMEM((groups, 8, LANES), jnp.int32),
                pltpu.VMEM((groups, 8, LANES), jnp.int32),
                pltpu.VMEM((groups, slots * 16, WIDE), bf16),
                pltpu.VMEM((groups, slots * 16, WIDE), bf16),
                pltpu.SMEM(pair_remote.shape, jnp.int32),
                pltpu.SMEM(pair_local.shape, jnp.int32),
                pltpu.SMEM(pair_count.shape, jnp.int32),
                pltpu.SemaphoreType.DMA((4,)),
                pltpu.SemaphoreType.DMA((5,)),
                pltpu.SemaphoreType.DMA((sends,)),
                pltpu.SemaphoreType.DMA((n_dev,)),
                pltpu.SemaphoreType.DMA((groups,)),
                pltpu.SemaphoreType.DMA((groups,)),
                pltpu.SemaphoreType.DMA((groups,)),
                pltpu.SemaphoreType.DMA((groups,)),
            ],
            compiler_params=pltpu.CompilerParams(
                collective_id=0, has_side_effects=True, vmem_limit_bytes=48 << 20
            ),
        )(source_pick, *held)
        return pl.pallas_call(
            functools.partial(store, n_dev),
            out_shape=(
                jax.ShapeDtypeStruct((channels, n_dev, LAGS), f32),
                jax.ShapeDtypeStruct(cross_shape, f32),
            ),
            in_specs=[anywhere, anywhere],
            out_specs=(anywhere, anywhere),
            scratch_shapes=[pltpu.SemaphoreType.DMA((channels + 1,))],
            compiler_params=pltpu.CompilerParams(vmem_limit_bytes=1 << 20),
        )(acc.reshape(total // channels, channels, LAGS), cross)

    return jax.shard_map(
        on_device,
        mesh=mesh,
        in_specs=(
            P(("grp", "dev"), None, None, None),
            P(("grp", "dev")),
            P("grp", "dev", None, None),
            P("grp", "dev", None, None),
            P("grp", "dev", None),
        ),
        out_specs=(P(("grp", "dev"), None, None), P("grp", "dev", None, None, None)),
        check_vma=False,
    )


def rows_of(n_dev):
    return n_dev // 4
```

```python
import functools

import jax
import jax.numpy as jnp
import numpy as np
from jax import lax
from jax.experimental import pallas as pl
from jax.experimental.pallas import tpu as pltpu
from jax.sharding import PartitionSpec as P

MESH = pl.DeviceIdType.MESH
F = 4096
LAGS = 512
HALF = LAGS // 2
BAND = 64
CHUNKS = 4
DIRECT = 2
WIDE = F // CHUNKS
LANES = 128
INNER = 256
BLK = F // INNER
SCALE = 0.5 * F ** (-0.5)
f32, bf16 = jnp.float32, jnp.bfloat16


def lag_tables():
    lag = np.arange(HALF)
    lag[0] = HALF
    angle = np.pi * ((np.arange(INNER)[:, None] * lag[None, :]) % (2 * F)) / F
    table = np.concatenate([np.cos(angle), np.sin(angle)], axis=1)
    turn = np.pi * ((np.arange(BLK)[:, None] * np.arange(LANES)[None, :]) % (2 * BLK)) / BLK
    turn = SCALE * np.stack([np.cos(turn), np.sin(turn)])
    return table.astype(jnp.bfloat16), np.repeat(turn[:, :, None, :], 8, axis=2).astype(np.float32)


def kernel(
    groups, n_dev, slots, channels,
    pick_ref, remote_hbm, local_hbm, count_hbm, x_hbm, table_hbm, turn_hbm,
    acc, cross_out,
    raw, white, mag, gathered, row_scratch, src_f32, x, y, table, turn, pr, pi,
    req_out, req_in, rows_out, rows_in, remote_ref, local_ref, count_ref,
    load_sem, small_sem, send_sem, recv_sem, req_send, req_recv, row_send, row_recv,
):
    g = lax.axis_index("grp")
    d = lax.axis_index("dev")
    rows = n_dev // 4
    r, c, k = d // 4, (d // 2) % 2, d % 2
    flip_k = r * 4 + c * 2 + (1 - k)
    across = [r * 4 + (1 - c) * 2 + k, r * 4 + (1 - c) * 2 + (1 - k)]

    def row_of(t):
        if rows == 4:
            return [r, r + 1 - 2 * (r % 2), 2 - r // 2, 3 - 3 * (r // 2)][t]
        return lax.rem(r + t, rows)

    def group_of(t):
        return lax.rem(g + t, groups)

    loads = [
        pltpu.make_async_copy(x_hbm.at[:, sp // 2, sp % 2, :], raw.at[sp], load_sem.at[sp]) for sp in range(4)
    ]
    remote_load = pltpu.make_async_copy(remote_hbm, remote_ref, small_sem.at[0])
    local_load = pltpu.make_async_copy(local_hbm, local_ref, small_sem.at[1])
    count_load = pltpu.make_async_copy(count_hbm, count_ref, small_sem.at[2])
    table_load = pltpu.make_async_copy(table_hbm, table, small_sem.at[3])
    turn_load = pltpu.make_async_copy(turn_hbm, turn, small_sem.at[4])
    for copy in loads + [remote_load, local_load, count_load, table_load, turn_load]:
        copy.start()

    barrier = pltpu.get_barrier_semaphore()
    for t in range(1, rows):
        pl.semaphore_signal(barrier, inc=1, device_id=(g, row_of(t) * 4 + c * 2 + k), device_id_type=MESH)
    for target in across + [flip_k]:
        pl.semaphore_signal(barrier, inc=1, device_id=(g, target), device_id_type=MESH)
    for row in range(rows - DIRECT, rows):
        @pl.when(r + c == 0)
        def _():
            pl.semaphore_signal(barrier, inc=1, device_id=(g, row * 4 + across[0] % 4), device_id_type=MESH)
    for t in range(1, groups):
        pl.semaphore_signal(barrier, inc=1, device_id=(group_of(t), d), device_id_type=MESH)

    started = []

    def remote(src, dst, send, recv, target):
        return pltpu.make_async_remote_copy(
            src_ref=src, dst_ref=dst, send_sem=send, recv_sem=recv, device_id=target, device_id_type=MESH
        )

    lane_i = lax.broadcasted_iota(jnp.int32, (LANES, LANES), 0)
    lane_j = lax.broadcasted_iota(jnp.int32, (LANES, LANES), 1)
    averaging = jnp.where(lane_i // BAND == lane_j // BAND, 1.0 / BAND, 0.0).astype(bf16)
    tiles = F // LANES

    def whiten():
        for s in range(2):
            for l in range(tiles):
                cols = slice(l * LANES, (l + 1) * LANES)
                re, im = raw[2 * s, :, cols], raw[2 * s + 1, :, cols]
                mag[(s * tiles + l) * channels:(s * tiles + l + 1) * channels, :] = jnp.sqrt(re * re + im * im)
        value = mag[...]
        high = value.astype(bf16)
        rest = value - high.astype(f32)
        mid = rest.astype(bf16)
        low = (rest - mid.astype(f32)).astype(bf16)
        mean = (
            jnp.dot(high, averaging, preferred_element_type=f32)
            + jnp.dot(mid, averaging, preferred_element_type=f32)
            + jnp.dot(low, averaging, preferred_element_type=f32)
        )
        mag[...] = 1.0 / (mean + 1e-05)
        for s in range(2):
            for l in range(tiles):
                cols = slice(l * LANES, (l + 1) * LANES)
                inverse = mag[(s * tiles + l) * channels:(s * tiles + l + 1) * channels, :]
                for p in range(2):
                    scaled = raw[2 * s + p, :, cols] * inverse
                    white[2 * s + p, :, cols] = scaled.astype(bf16).astype(f32)

    def pick_row(channel):
        for sp in range(4):
            for i in range(CHUNKS):
                row_scratch[sp * CHUNKS + i:sp * CHUNKS + i + 1, :] = white[
                    sp, pl.ds(channel, 1), i * WIDE:(i + 1) * WIDE
                ]

    n_sent = [0]

    def forward(j, target, when=None):
        copy = remote(gathered.at[j], gathered.at[j], send_sem.at[n_sent[0]], recv_sem.at[j], (g, target))
        n_sent[0] += 1
        if when is None:
            copy.start()
        else:
            pl.when(when)(copy.start)
        started.append((when, copy))

    def arrived(j):
        remote(gathered.at[j], gathered.at[j], send_sem.at[0], recv_sem.at[j], (g, flip_k)).wait_recv()

    def transform(bases, zeros):
        used = 2 * HALF * len(bases)
        y[0:used, :] = jnp.dot(x[0:used, :], table[...], preferred_element_type=f32)
        for n, (base, zero) in enumerate(zip(bases, zeros)):
            turn_back(n * 2 * HALF, base, zero)

    def turn_back(row, base, zero):
        for h in range(2):
            p = [jnp.zeros((8, LANES), f32) for _ in range(2)]
            q = [jnp.zeros((8, LANES), f32) for _ in range(2)]
            for b in range(BLK):
                cos, sin = turn[0, b], turn[1, b]
                real = slice(row + b * 16 + h * 8, row + b * 16 + h * 8 + 8)
                imag = slice(row + HALF + b * 16 + h * 8, row + HALF + b * 16 + h * 8 + 8)
                for u in range(2):
                    on_cos = slice(u * LANES, (u + 1) * LANES)
                    on_sin = slice(HALF + u * LANES, HALF + (u + 1) * LANES)
                    p[u] = p[u] + (cos * y[real, on_cos] - sin * y[real, on_sin])
                    q[u] = q[u] + (cos * y[imag, on_sin] + sin * y[imag, on_cos])
            lane = lax.broadcasted_iota(jnp.int32, (8, LANES), 1)
            back = lax.rem(LANES - lane, LANES)
            turned = [jnp.take_along_axis(p[u] + q[u], back, axis=1) for u in range(2)]
            out = [
                jnp.where(lane == 0, turned[0], turned[1]),
                jnp.where(lane == 0, turned[1], turned[0]),
                jnp.where(lane == 0, zero[h] * SCALE, p[0] - q[0]),
                p[1] - q[1],
            ]
            for n in range(4):
                acc[pl.ds(base + h * 8, 8), n * LANES:(n + 1) * LANES] = out[n]

    def cross(first, n):
        for half in range(2):
            src_f32[2 * n + half] = gathered[first + half].astype(f32)
        total = [jnp.zeros((channels, LANES), f32) for _ in range(2)]
        for l in range(tiles):
            i, lanes = l // 8, slice(l % 8 * LANES, (l % 8 + 1) * LANES)
            w = [white[sp, :, l * LANES:(l + 1) * LANES] for sp in range(4)]
            real, imag = [], []
            for half in range(2):
                v = [
                    jnp.broadcast_to(
                        src_f32[2 * n + half, sp * CHUNKS + i:sp * CHUNKS + i + 1, lanes], (channels, LANES)
                    )
                    for sp in range(4)
                ]
                real.append(w[0] * v[0] + w[1] * v[1] + w[2] * v[2] + w[3] * v[3])
                imag.append(w[1] * v[0] - w[0] * v[1] + w[3] * v[2] - w[2] * v[3])
                total[half] = total[half] + real[-1]
            b, cols = l // 2, slice(l % 2 * LANES, (l % 2 + 1) * LANES)
            row = 2 * HALF * n + b * 16
            x[row:row + 16, cols] = jnp.concatenate(real, axis=0).astype(bf16)
            x[HALF + row:HALF + row + 16, cols] = jnp.concatenate(imag, axis=0).astype(bf16)
        return [jnp.sum(t, axis=1, keepdims=True) for t in total]

    def batch(*firsts):
        zeros = [cross(first, n) for n, first in enumerate(firsts)]
        transform([pl.multiple_of(first * channels, 2 * channels) for first in firsts], zeros)

    for copy in loads:
        copy.wait()
    whiten()
    pick_row(pick_ref[0])
    gathered[d] = row_scratch[...].astype(bf16)
    remote_load.wait()
    for t in range(1, groups):
        h = group_of(t)
        for slot in range(slots):
            req_out[t, slot:slot + 1, :] = jnp.full((1, LANES), remote_ref[0, 0, h, slot], jnp.int32)

    pl.semaphore_wait(barrier, rows + 2 + groups - 1 + (r + DIRECT) // rows * c)
    straight = (r >= rows - DIRECT) & (c == 1)
    forward(d, across[0] % 4, straight)
    for t in range(rows - 1, 0, -1):
        forward(d, row_of(t) * 4 + c * 2 + k)
    for target in [flip_k] + across:
        forward(d, target)
    for t in range(1, groups):
        copy = remote(req_out.at[t], req_in.at[g], req_send.at[t], req_recv.at[g], (group_of(t), d))
        copy.start()
        started.append((None, copy))

    table_load.wait()
    turn_load.wait()
    arrived(flip_k)
    batch(r * 4 + c * 2)

    channel_id = lax.broadcasted_iota(jnp.int32, (channels, LANES), 0)
    for t in range(1, groups):
        h = group_of(t)
        remote(req_out.at[t], req_in.at[h], req_send.at[t], req_recv.at[h], (h, d)).wait_recv()
        asked = req_in[h]
        for slot in range(slots):
            chosen = channel_id == jnp.broadcast_to(asked[slot:slot + 1, :], (channels, LANES))
            chosen = jnp.concatenate([chosen] * (WIDE // LANES), axis=1)
            for sp in range(4):
                for q in range(CHUNKS):
                    part = jnp.where(chosen, white[sp, :, q * WIDE:(q + 1) * WIDE], 0.0)
                    row_scratch[sp * CHUNKS + q:sp * CHUNKS + q + 1, :] = jnp.sum(part, axis=0, keepdims=True)
            rows_out[t, slot * 16:(slot + 1) * 16, :] = row_scratch[...].astype(bf16)
        copy = remote(rows_out.at[t], rows_in.at[g], row_send.at[t], row_recv.at[g], (h, d))
        copy.start()
        started.append((None, copy))

    for t in range(1, rows):
        j = row_of(t) * 4 + c * 2 + k
        arrived(j)
        for target in across:
            forward(j, target, (r > 0) | (c == 0) if t >= rows - DIRECT else None)
        forward(j, flip_k)

    def near(t):
        first = row_of(t) * 4 + c * 2
        arrived(first + (1 - k))
        return first

    def far(t):
        first = row_of(t) * 4 + (1 - c) * 2
        arrived(first + (1 - k))
        pl.when(jnp.logical_or(r + c > 0, row_of(t) < rows - DIRECT))(functools.partial(arrived, first + k))
        return first

    def in_twos(wait, first_t, end_t):
        if (end_t - first_t) % 2:
            batch(wait(first_t))
            first_t += 1
        for t in range(first_t, end_t, 2):
            batch(wait(t), wait(t + 1))

    batch(far(0), near(1))
    for row in range(rows - DIRECT, rows):
        j = row * 4 + across[0] % 4
        pl.when(r + c == 0)(functools.partial(arrived, j))
        forward(j, flip_k, r + c == 0)

    in_twos(near, 2, rows)

    local_load.wait()
    count_load.wait()
    cross_out[0, 0, g] = jnp.zeros((slots, LAGS), f32)
    pairs = (groups - 1) * slots
    for base in range(0, pairs, 16):
        pr[...] = jnp.zeros_like(pr)
        pi[...] = jnp.zeros_like(pi)
        for n in range(base, min(base + 16, pairs)):
            t, slot = n // slots + 1, n % slots
            h = group_of(t)
            if slot == 0:
                remote(rows_out.at[t], rows_in.at[h], row_send.at[t], row_recv.at[h], (h, d)).wait_recv()
            pick_row(local_ref[0, 0, h, slot])
            there = rows_in[h, slot * 16:(slot + 1) * 16, :].astype(f32)
            here = row_scratch[...]
            w = [here[sp * CHUNKS:(sp + 1) * CHUNKS] for sp in range(4)]
            v = [there[sp * CHUNKS:(sp + 1) * CHUNKS] for sp in range(4)]
            real = w[0] * v[0] + w[1] * v[1] + w[2] * v[2] + w[3] * v[3]
            imag = w[1] * v[0] - w[0] * v[1] + w[3] * v[2] - w[2] * v[3]
            for q in range(CHUNKS):
                pr[n - base:n - base + 1, q * WIDE:(q + 1) * WIDE] = real[q:q + 1]
                pi[n - base:n - base + 1, q * WIDE:(q + 1) * WIDE] = imag[q:q + 1]
        for b in range(BLK):
            x[b * 16:(b + 1) * 16, :] = pr[:, b * INNER:(b + 1) * INNER].astype(bf16)
            x[HALF + b * 16:HALF + (b + 1) * 16, :] = pi[:, b * INNER:(b + 1) * INNER].astype(bf16)
        zero = [jnp.sum(pr[h * 8:(h + 1) * 8, :], axis=1, keepdims=True) for h in range(2)]
        transform([n_dev * channels], [zero])
        for n in range(base, min(base + 16, pairs)):
            t, slot = n // slots + 1, n % slots
            h = group_of(t)
            row = n_dev * channels + n - base
            keep = jnp.where(slot < count_ref[0, 0, h], 1.0, 0.0)
            cross_out[0, 0, h, slot:slot + 1, :] = acc[row:row + 1, :] * keep

    in_twos(far, 1, rows - 1)
    batch(far(rows - 1))

    for when, copy in started:
        if when is None:
            copy.wait_send()
        else:
            pl.when(when)(copy.wait_send)


def store(n_dev, acc, cross_in, group_out, cross_out, sem):
    channels = group_out.shape[0]
    copies = [
        pltpu.make_async_copy(acc.at[0:n_dev, ch, :], group_out.at[ch], sem.at[ch]) for ch in range(channels)
    ] + [pltpu.make_async_copy(cross_in, cross_out, sem.at[channels])]
    for copy in copies:
        copy.start()
    for copy in copies:
        copy.wait()


def solution(mesh):
    groups, n_dev = mesh.shape["grp"], mesh.shape["dev"]
    table, turn = lag_tables()

    def on_device(spectra, source_pick, pair_remote, pair_local, pair_count):
        channels = spectra.shape[0]
        slots = pair_remote.shape[3]
        total = n_dev * channels + 16
        hbm = pl.BlockSpec(memory_space=pltpu.HBM)
        vmem = pl.BlockSpec(memory_space=pltpu.VMEM)
        anywhere = pl.BlockSpec(memory_space=pl.ANY)
        held = [
            pltpu.with_memory_space_constraint(a, pltpu.HBM)
            for a in (pair_remote, pair_local, pair_count, spectra, jnp.asarray(table), jnp.asarray(turn))
        ]
        cross_shape = (1, 1, groups, slots, LAGS)
        sends = DIRECT + 2 + 3 * rows_of(n_dev) + rows_of(n_dev) - 1
        acc, cross = pl.pallas_call(
            functools.partial(kernel, groups, n_dev, slots, channels),
            out_shape=(pltpu.VMEM((total, LAGS), f32), pltpu.VMEM(cross_shape, f32)),
            in_specs=[pl.BlockSpec(memory_space=pltpu.SMEM)] + [hbm] * 6,
            out_specs=(vmem, vmem),
            scratch_shapes=[
                pltpu.VMEM((4, channels, F), f32),
                pltpu.VMEM((4, channels, F), f32),
                pltpu.VMEM((2 * F // LANES * channels, LANES), f32),
                pltpu.VMEM((n_dev, 16, WIDE), bf16),
                pltpu.VMEM((16, WIDE), f32),
                pltpu.VMEM((4, 16, WIDE), f32),
                pltpu.VMEM((4 * HALF, INNER), bf16),
                pltpu.VMEM((4 * HALF, 2 * HALF), f32),
                pltpu.VMEM(table.shape, bf16),
                pltpu.VMEM(turn.shape, f32),
                pltpu.VMEM((16, F), f32),
                pltpu.VMEM((16, F), f32),
                pltpu.VMEM((groups, 8, LANES), jnp.int32),
                pltpu.VMEM((groups, 8, LANES), jnp.int32),
                pltpu.VMEM((groups, slots * 16, WIDE), bf16),
                pltpu.VMEM((groups, slots * 16, WIDE), bf16),
                pltpu.SMEM(pair_remote.shape, jnp.int32),
                pltpu.SMEM(pair_local.shape, jnp.int32),
                pltpu.SMEM(pair_count.shape, jnp.int32),
                pltpu.SemaphoreType.DMA((4,)),
                pltpu.SemaphoreType.DMA((5,)),
                pltpu.SemaphoreType.DMA((sends,)),
                pltpu.SemaphoreType.DMA((n_dev,)),
                pltpu.SemaphoreType.DMA((groups,)),
                pltpu.SemaphoreType.DMA((groups,)),
                pltpu.SemaphoreType.DMA((groups,)),
                pltpu.SemaphoreType.DMA((groups,)),
            ],
            compiler_params=pltpu.CompilerParams(
                collective_id=0, has_side_effects=True, vmem_limit_bytes=48 << 20
            ),
        )(source_pick, *held)
        return pl.pallas_call(
            functools.partial(store, n_dev),
            out_shape=(
                jax.ShapeDtypeStruct((channels, n_dev, LAGS), f32),
                jax.ShapeDtypeStruct(cross_shape, f32),
            ),
            in_specs=[anywhere, anywhere],
            out_specs=(anywhere, anywhere),
            scratch_shapes=[pltpu.SemaphoreType.DMA((channels + 1,))],
            compiler_params=pltpu.CompilerParams(vmem_limit_bytes=1 << 20),
        )(acc.reshape(total // channels, channels, LAGS), cross)

    return jax.shard_map(
        on_device,
        mesh=mesh,
        in_specs=(
            P(("grp", "dev"), None, None, None),
            P(("grp", "dev")),
            P("grp", "dev", None, None),
            P("grp", "dev", None, None),
            P("grp", "dev", None),
        ),
        out_specs=(P(("grp", "dev"), None, None), P("grp", "dev", None, None, None)),
        check_vma=False,
    )


def rows_of(n_dev):
    return n_dev // 4
```

```python
import functools

import jax
import jax.numpy as jnp
import numpy as np
from jax import lax
from jax.experimental import pallas as pl
from jax.experimental.pallas import tpu as pltpu
from jax.sharding import PartitionSpec as P

MESH = pl.DeviceIdType.MESH
F = 4096
LAGS = 512
HALF = LAGS // 2
BAND = 64
CHUNKS = 4
DIRECT = 2
WIDE = F // CHUNKS
LANES = 128
INNER = 256
BLK = F // INNER
SCALE = 0.5 * F ** (-0.5)
f32, bf16 = jnp.float32, jnp.bfloat16


def lag_tables():
    lag = np.arange(HALF)
    lag[0] = HALF
    angle = np.pi * ((np.arange(INNER)[:, None] * lag[None, :]) % (2 * F)) / F
    table = np.concatenate([np.cos(angle), np.sin(angle)], axis=1)
    turn = np.pi * ((np.arange(BLK)[:, None] * np.arange(LANES)[None, :]) % (2 * BLK)) / BLK
    turn = SCALE * np.stack([np.cos(turn), np.sin(turn)])
    return table.astype(jnp.bfloat16), np.repeat(turn[:, :, None, :], 8, axis=2).astype(np.float32)


def kernel(
    groups, n_dev, slots, channels,
    pick_ref, remote_hbm, local_hbm, count_hbm, x_hbm, table_hbm, turn_hbm,
    acc, cross_out,
    raw, white, mag, gathered, row_scratch, src_f32, x, y, table, turn, pr, pi,
    req_out, req_in, rows_out, rows_in, remote_ref, local_ref, count_ref,
    load_sem, small_sem, send_sem, recv_sem, req_send, req_recv, row_send, row_recv,
):
    g = lax.axis_index("grp")
    d = lax.axis_index("dev")
    rows = n_dev // 4
    r, c, k = d // 4, (d // 2) % 2, d % 2
    flip_k = r * 4 + c * 2 + (1 - k)
    across = [r * 4 + (1 - c) * 2 + k, r * 4 + (1 - c) * 2 + (1 - k)]

    def row_of(t):
        if rows == 4:
            return [r, r + 1 - 2 * (r % 2), 2 - r // 2, 3 - 3 * (r // 2)][t]
        return lax.rem(r + t, rows)

    def group_of(t):
        return lax.rem(g + t, groups)

    loads = [
        pltpu.make_async_copy(x_hbm.at[:, sp // 2, sp % 2, :], raw.at[sp], load_sem.at[sp]) for sp in range(4)
    ]
    remote_load = pltpu.make_async_copy(remote_hbm, remote_ref, small_sem.at[0])
    local_load = pltpu.make_async_copy(local_hbm, local_ref, small_sem.at[1])
    count_load = pltpu.make_async_copy(count_hbm, count_ref, small_sem.at[2])
    table_load = pltpu.make_async_copy(table_hbm, table, small_sem.at[3])
    turn_load = pltpu.make_async_copy(turn_hbm, turn, small_sem.at[4])
    for copy in loads + [remote_load, local_load, count_load, table_load, turn_load]:
        copy.start()

    barrier = pltpu.get_barrier_semaphore()
    for t in range(1, rows):
        pl.semaphore_signal(barrier, inc=1, device_id=(g, row_of(t) * 4 + c * 2 + k), device_id_type=MESH)
    for target in across + [flip_k]:
        pl.semaphore_signal(barrier, inc=1, device_id=(g, target), device_id_type=MESH)
    for row in range(rows - DIRECT, rows):
        @pl.when(r + c + g == 0)
        def _():
            pl.semaphore_signal(barrier, inc=1, device_id=(g, row * 4 + across[0] % 4), device_id_type=MESH)
    for t in range(1, groups):
        pl.semaphore_signal(barrier, inc=1, device_id=(group_of(t), d), device_id_type=MESH)

    started = []

    def remote(src, dst, send, recv, target):
        return pltpu.make_async_remote_copy(
            src_ref=src, dst_ref=dst, send_sem=send, recv_sem=recv, device_id=target, device_id_type=MESH
        )

    lane_i = lax.broadcasted_iota(jnp.int32, (LANES, LANES), 0)
    lane_j = lax.broadcasted_iota(jnp.int32, (LANES, LANES), 1)
    averaging = jnp.where(lane_i // BAND == lane_j // BAND, 1.0 / BAND, 0.0).astype(bf16)
    tiles = F // LANES

    def whiten():
        for s in range(2):
            for l in range(tiles):
                cols = slice(l * LANES, (l + 1) * LANES)
                re, im = raw[2 * s, :, cols], raw[2 * s + 1, :, cols]
                mag[(s * tiles + l) * channels:(s * tiles + l + 1) * channels, :] = jnp.sqrt(re * re + im * im)
        value = mag[...]
        high = value.astype(bf16)
        rest = value - high.astype(f32)
        mid = rest.astype(bf16)
        low = (rest - mid.astype(f32)).astype(bf16)
        mean = (
            jnp.dot(high, averaging, preferred_element_type=f32)
            + jnp.dot(mid, averaging, preferred_element_type=f32)
            + jnp.dot(low, averaging, preferred_element_type=f32)
        )
        mag[...] = 1.0 / (mean + 1e-05)
        for s in range(2):
            for l in range(tiles):
                cols = slice(l * LANES, (l + 1) * LANES)
                inverse = mag[(s * tiles + l) * channels:(s * tiles + l + 1) * channels, :]
                for p in range(2):
                    scaled = raw[2 * s + p, :, cols] * inverse
                    white[2 * s + p, :, cols] = scaled.astype(bf16).astype(f32)

    def pick_row(channel):
        for sp in range(4):
            for i in range(CHUNKS):
                row_scratch[sp * CHUNKS + i:sp * CHUNKS + i + 1, :] = white[
                    sp, pl.ds(channel, 1), i * WIDE:(i + 1) * WIDE
                ]

    n_sent = [0]

    def forward(j, target, when=None):
        copy = remote(gathered.at[j], gathered.at[j], send_sem.at[n_sent[0]], recv_sem.at[j], (g, target))
        n_sent[0] += 1
        if when is None:
            copy.start()
        else:
            pl.when(when)(copy.start)
        started.append((when, copy))

    def arrived(j):
        remote(gathered.at[j], gathered.at[j], send_sem.at[0], recv_sem.at[j], (g, flip_k)).wait_recv()

    def transform(bases, zeros):
        used = 2 * HALF * len(bases)
        y[0:used, :] = jnp.dot(x[0:used, :], table[...], preferred_element_type=f32)
        for n, (base, zero) in enumerate(zip(bases, zeros)):
            turn_back(n * 2 * HALF, base, zero)

    def turn_back(row, base, zero):
        for h in range(2):
            p = [jnp.zeros((8, LANES), f32) for _ in range(2)]
            q = [jnp.zeros((8, LANES), f32) for _ in range(2)]
            for b in range(BLK):
                cos, sin = turn[0, b], turn[1, b]
                real = slice(row + b * 16 + h * 8, row + b * 16 + h * 8 + 8)
                imag = slice(row + HALF + b * 16 + h * 8, row + HALF + b * 16 + h * 8 + 8)
                for u in range(2):
                    on_cos = slice(u * LANES, (u + 1) * LANES)
                    on_sin = slice(HALF + u * LANES, HALF + (u + 1) * LANES)
                    p[u] = p[u] + (cos * y[real, on_cos] - sin * y[real, on_sin])
                    q[u] = q[u] + (cos * y[imag, on_sin] + sin * y[imag, on_cos])
            lane = lax.broadcasted_iota(jnp.int32, (8, LANES), 1)
            back = lax.rem(LANES - lane, LANES)
            turned = [jnp.take_along_axis(p[u] + q[u], back, axis=1) for u in range(2)]
            out = [
                jnp.where(lane == 0, turned[0], turned[1]),
                jnp.where(lane == 0, turned[1], turned[0]),
                jnp.where(lane == 0, zero[h] * SCALE, p[0] - q[0]),
                p[1] - q[1],
            ]
            for n in range(4):
                acc[pl.ds(base + h * 8, 8), n * LANES:(n + 1) * LANES] = out[n]

    def cross(first, n):
        for half in range(2):
            src_f32[2 * n + half] = gathered[first + half].astype(f32)
        total = [jnp.zeros((channels, LANES), f32) for _ in range(2)]
        for l in range(tiles):
            i, lanes = l // 8, slice(l % 8 * LANES, (l % 8 + 1) * LANES)
            w = [white[sp, :, l * LANES:(l + 1) * LANES] for sp in range(4)]
            real, imag = [], []
            for half in range(2):
                v = [
                    jnp.broadcast_to(
                        src_f32[2 * n + half, sp * CHUNKS + i:sp * CHUNKS + i + 1, lanes], (channels, LANES)
                    )
                    for sp in range(4)
                ]
                real.append(w[0] * v[0] + w[1] * v[1] + w[2] * v[2] + w[3] * v[3])
                imag.append(w[1] * v[0] - w[0] * v[1] + w[3] * v[2] - w[2] * v[3])
                total[half] = total[half] + real[-1]
            b, cols = l // 2, slice(l % 2 * LANES, (l % 2 + 1) * LANES)
            row = 2 * HALF * n + b * 16
            x[row:row + 16, cols] = jnp.concatenate(real, axis=0).astype(bf16)
            x[HALF + row:HALF + row + 16, cols] = jnp.concatenate(imag, axis=0).astype(bf16)
        return [jnp.sum(t, axis=1, keepdims=True) for t in total]

    def batch(*firsts):
        zeros = [cross(first, n) for n, first in enumerate(firsts)]
        transform([pl.multiple_of(first * channels, 2 * channels) for first in firsts], zeros)

    for copy in loads:
        copy.wait()
    whiten()
    pick_row(pick_ref[0])
    gathered[d] = row_scratch[...].astype(bf16)
    remote_load.wait()
    for t in range(1, groups):
        h = group_of(t)
        for slot in range(slots):
            req_out[t, slot:slot + 1, :] = jnp.full((1, LANES), remote_ref[0, 0, h, slot], jnp.int32)

    pl.semaphore_wait(barrier, rows + 2 + groups - 1 + (r + DIRECT) // rows * c * (g == 0))
    straight = (r >= rows - DIRECT) & (c == 1) & (g == 0)
    forward(d, across[0] % 4, straight)
    for t in range(rows - 1, 0, -1):
        forward(d, row_of(t) * 4 + c * 2 + k)
    for target in [flip_k] + across:
        forward(d, target)
    for t in range(1, groups):
        copy = remote(req_out.at[t], req_in.at[g], req_send.at[t], req_recv.at[g], (group_of(t), d))
        copy.start()
        started.append((None, copy))

    table_load.wait()
    turn_load.wait()
    arrived(flip_k)
    batch(r * 4 + c * 2)

    channel_id = lax.broadcasted_iota(jnp.int32, (channels, LANES), 0)
    for t in range(1, groups):
        h = group_of(t)
        remote(req_out.at[t], req_in.at[h], req_send.at[t], req_recv.at[h], (h, d)).wait_recv()
        asked = req_in[h]
        for slot in range(slots):
            chosen = channel_id == jnp.broadcast_to(asked[slot:slot + 1, :], (channels, LANES))
            chosen = jnp.concatenate([chosen] * (WIDE // LANES), axis=1)
            for sp in range(4):
                for q in range(CHUNKS):
                    part = jnp.where(chosen, white[sp, :, q * WIDE:(q + 1) * WIDE], 0.0)
                    row_scratch[sp * CHUNKS + q:sp * CHUNKS + q + 1, :] = jnp.sum(part, axis=0, keepdims=True)
            rows_out[t, slot * 16:(slot + 1) * 16, :] = row_scratch[...].astype(bf16)
        copy = remote(rows_out.at[t], rows_in.at[g], row_send.at[t], row_recv.at[g], (h, d))
        copy.start()
        started.append((None, copy))

    for t in range(1, rows):
        j = row_of(t) * 4 + c * 2 + k
        arrived(j)
        for target in across:
            forward(j, target, (r > 0) | (c == 0) | (g > 0) if t >= rows - DIRECT else None)
        forward(j, flip_k)

    def near(t):
        first = row_of(t) * 4 + c * 2
        arrived(first + (1 - k))
        return first

    def far(t):
        first = row_of(t) * 4 + (1 - c) * 2
        arrived(first + (1 - k))
        pl.when(jnp.logical_or(r + c + g > 0, row_of(t) < rows - DIRECT))(functools.partial(arrived, first + k))
        return first

    def in_twos(wait, first_t, end_t):
        if (end_t - first_t) % 2:
            batch(wait(first_t))
            first_t += 1
        for t in range(first_t, end_t, 2):
            batch(wait(t), wait(t + 1))

    batch(far(0), near(1))
    for row in range(rows - DIRECT, rows):
        j = row * 4 + across[0] % 4
        pl.when(r + c + g == 0)(functools.partial(arrived, j))
        forward(j, flip_k, r + c + g == 0)

    in_twos(near, 2, rows)

    local_load.wait()
    count_load.wait()
    cross_out[0, 0, g] = jnp.zeros((slots, LAGS), f32)
    pairs = (groups - 1) * slots
    for base in range(0, pairs, 16):
        pr[...] = jnp.zeros_like(pr)
        pi[...] = jnp.zeros_like(pi)
        for n in range(base, min(base + 16, pairs)):
            t, slot = n // slots + 1, n % slots
            h = group_of(t)
            if slot == 0:
                remote(rows_out.at[t], rows_in.at[h], row_send.at[t], row_recv.at[h], (h, d)).wait_recv()
            pick_row(local_ref[0, 0, h, slot])
            there = rows_in[h, slot * 16:(slot + 1) * 16, :].astype(f32)
            here = row_scratch[...]
            w = [here[sp * CHUNKS:(sp + 1) * CHUNKS] for sp in range(4)]
            v = [there[sp * CHUNKS:(sp + 1) * CHUNKS] for sp in range(4)]
            real = w[0] * v[0] + w[1] * v[1] + w[2] * v[2] + w[3] * v[3]
            imag = w[1] * v[0] - w[0] * v[1] + w[3] * v[2] - w[2] * v[3]
            for q in range(CHUNKS):
                pr[n - base:n - base + 1, q * WIDE:(q + 1) * WIDE] = real[q:q + 1]
                pi[n - base:n - base + 1, q * WIDE:(q + 1) * WIDE] = imag[q:q + 1]
        for b in range(BLK):
            x[b * 16:(b + 1) * 16, :] = pr[:, b * INNER:(b + 1) * INNER].astype(bf16)
            x[HALF + b * 16:HALF + (b + 1) * 16, :] = pi[:, b * INNER:(b + 1) * INNER].astype(bf16)
        zero = [jnp.sum(pr[h * 8:(h + 1) * 8, :], axis=1, keepdims=True) for h in range(2)]
        transform([n_dev * channels], [zero])
        for n in range(base, min(base + 16, pairs)):
            t, slot = n // slots + 1, n % slots
            h = group_of(t)
            row = n_dev * channels + n - base
            keep = jnp.where(slot < count_ref[0, 0, h], 1.0, 0.0)
            cross_out[0, 0, h, slot:slot + 1, :] = acc[row:row + 1, :] * keep

    in_twos(far, 1, rows - 1)
    batch(far(rows - 1))

    for when, copy in started:
        if when is None:
            copy.wait_send()
        else:
            pl.when(when)(copy.wait_send)


def store(n_dev, acc, cross_in, group_out, cross_out, sem):
    channels = group_out.shape[0]
    copies = [
        pltpu.make_async_copy(acc.at[0:n_dev, ch, :], group_out.at[ch], sem.at[ch]) for ch in range(channels)
    ] + [pltpu.make_async_copy(cross_in, cross_out, sem.at[channels])]
    for copy in copies:
        copy.start()
    for copy in copies:
        copy.wait()


def solution(mesh):
    groups, n_dev = mesh.shape["grp"], mesh.shape["dev"]
    table, turn = lag_tables()

    def on_device(spectra, source_pick, pair_remote, pair_local, pair_count):
        channels = spectra.shape[0]
        slots = pair_remote.shape[3]
        total = n_dev * channels + 16
        hbm = pl.BlockSpec(memory_space=pltpu.HBM)
        vmem = pl.BlockSpec(memory_space=pltpu.VMEM)
        anywhere = pl.BlockSpec(memory_space=pl.ANY)
        held = [
            pltpu.with_memory_space_constraint(a, pltpu.HBM)
            for a in (pair_remote, pair_local, pair_count, spectra, jnp.asarray(table), jnp.asarray(turn))
        ]
        cross_shape = (1, 1, groups, slots, LAGS)
        sends = DIRECT + 2 + 3 * rows_of(n_dev) + rows_of(n_dev) - 1
        acc, cross = pl.pallas_call(
            functools.partial(kernel, groups, n_dev, slots, channels),
            out_shape=(pltpu.VMEM((total, LAGS), f32), pltpu.VMEM(cross_shape, f32)),
            in_specs=[pl.BlockSpec(memory_space=pltpu.SMEM)] + [hbm] * 6,
            out_specs=(vmem, vmem),
            scratch_shapes=[
                pltpu.VMEM((4, channels, F), f32),
                pltpu.VMEM((4, channels, F), f32),
                pltpu.VMEM((2 * F // LANES * channels, LANES), f32),
                pltpu.VMEM((n_dev, 16, WIDE), bf16),
                pltpu.VMEM((16, WIDE), f32),
                pltpu.VMEM((4, 16, WIDE), f32),
                pltpu.VMEM((4 * HALF, INNER), bf16),
                pltpu.VMEM((4 * HALF, 2 * HALF), f32),
                pltpu.VMEM(table.shape, bf16),
                pltpu.VMEM(turn.shape, f32),
                pltpu.VMEM((16, F), f32),
                pltpu.VMEM((16, F), f32),
                pltpu.VMEM((groups, 8, LANES), jnp.int32),
                pltpu.VMEM((groups, 8, LANES), jnp.int32),
                pltpu.VMEM((groups, slots * 16, WIDE), bf16),
                pltpu.VMEM((groups, slots * 16, WIDE), bf16),
                pltpu.SMEM(pair_remote.shape, jnp.int32),
                pltpu.SMEM(pair_local.shape, jnp.int32),
                pltpu.SMEM(pair_count.shape, jnp.int32),
                pltpu.SemaphoreType.DMA((4,)),
                pltpu.SemaphoreType.DMA((5,)),
                pltpu.SemaphoreType.DMA((sends,)),
                pltpu.SemaphoreType.DMA((n_dev,)),
                pltpu.SemaphoreType.DMA((groups,)),
                pltpu.SemaphoreType.DMA((groups,)),
                pltpu.SemaphoreType.DMA((groups,)),
                pltpu.SemaphoreType.DMA((groups,)),
            ],
            compiler_params=pltpu.CompilerParams(
                collective_id=0, has_side_effects=True, vmem_limit_bytes=48 << 20
            ),
        )(source_pick, *held)
        return pl.pallas_call(
            functools.partial(store, n_dev),
            out_shape=(
                jax.ShapeDtypeStruct((channels, n_dev, LAGS), f32),
                jax.ShapeDtypeStruct(cross_shape, f32),
            ),
            in_specs=[anywhere, anywhere],
            out_specs=(anywhere, anywhere),
            scratch_shapes=[pltpu.SemaphoreType.DMA((channels + 1,))],
            compiler_params=pltpu.CompilerParams(vmem_limit_bytes=1 << 20),
        )(acc.reshape(total // channels, channels, LAGS), cross)

    return jax.shard_map(
        on_device,
        mesh=mesh,
        in_specs=(
            P(("grp", "dev"), None, None, None),
            P(("grp", "dev")),
            P("grp", "dev", None, None),
            P("grp", "dev", None, None),
            P("grp", "dev", None),
        ),
        out_specs=(P(("grp", "dev"), None, None), P("grp", "dev", None, None, None)),
        check_vma=False,
    )


def rows_of(n_dev):
    return n_dev // 4
```

```python
import functools

import jax
import jax.numpy as jnp
import numpy as np
from jax import lax
from jax.experimental import pallas as pl
from jax.experimental.pallas import tpu as pltpu
from jax.sharding import PartitionSpec as P

MESH = pl.DeviceIdType.MESH
F = 4096
LAGS = 512
HALF = LAGS // 2
BAND = 64
CHUNKS = 4
DIRECT = 2
WIDE = F // CHUNKS
LANES = 128
INNER = 256
BLK = F // INNER
SCALE = 0.5 * F ** (-0.5)
f32, bf16 = jnp.float32, jnp.bfloat16


def lag_tables():
    lag = np.arange(HALF)
    lag[0] = HALF
    angle = np.pi * ((np.arange(INNER)[:, None] * lag[None, :]) % (2 * F)) / F
    table = np.concatenate([np.cos(angle), np.sin(angle)], axis=1)
    turn = np.pi * ((np.arange(BLK)[:, None] * np.arange(LANES)[None, :]) % (2 * BLK)) / BLK
    turn = SCALE * np.stack([np.cos(turn), np.sin(turn)])
    return table.astype(jnp.bfloat16), np.repeat(turn[:, :, None, :], 8, axis=2).astype(np.float32)


def kernel(
    groups, n_dev, slots, channels,
    pick_ref, remote_hbm, local_hbm, count_hbm, x_hbm, table_hbm, turn_hbm,
    acc, cross_out,
    raw, white, mag, gathered, row_scratch, src_f32, x, y, table, turn, pr, pi, local_rows,
    req_out, req_in, rows_out, rows_in, remote_ref, local_ref, count_ref,
    load_sem, small_sem, send_sem, recv_sem, req_send, req_recv, row_send, row_recv,
):
    g = lax.axis_index("grp")
    d = lax.axis_index("dev")
    rows = n_dev // 4
    r, c, k = d // 4, (d // 2) % 2, d % 2
    flip_k = r * 4 + c * 2 + (1 - k)
    across = [r * 4 + (1 - c) * 2 + k, r * 4 + (1 - c) * 2 + (1 - k)]

    def row_of(t):
        if rows == 4:
            return [r, r + 1 - 2 * (r % 2), 2 - r // 2, 3 - 3 * (r // 2)][t]
        return lax.rem(r + t, rows)

    def group_of(t):
        return lax.rem(g + t, groups)

    loads = [
        pltpu.make_async_copy(x_hbm.at[:, sp // 2, sp % 2, :], raw.at[sp], load_sem.at[sp]) for sp in range(4)
    ]
    remote_load = pltpu.make_async_copy(remote_hbm, remote_ref, small_sem.at[0])
    local_load = pltpu.make_async_copy(local_hbm, local_ref, small_sem.at[1])
    count_load = pltpu.make_async_copy(count_hbm, count_ref, small_sem.at[2])
    table_load = pltpu.make_async_copy(table_hbm, table, small_sem.at[3])
    turn_load = pltpu.make_async_copy(turn_hbm, turn, small_sem.at[4])
    for copy in loads + [remote_load, local_load, count_load, table_load, turn_load]:
        copy.start()

    barrier = pltpu.get_barrier_semaphore()
    for t in range(1, rows):
        pl.semaphore_signal(barrier, inc=1, device_id=(g, row_of(t) * 4 + c * 2 + k), device_id_type=MESH)
    for target in across + [flip_k]:
        pl.semaphore_signal(barrier, inc=1, device_id=(g, target), device_id_type=MESH)
    for row in range(rows - DIRECT, rows):
        @pl.when(r + c + g == 0)
        def _():
            pl.semaphore_signal(barrier, inc=1, device_id=(g, row * 4 + across[0] % 4), device_id_type=MESH)
    for t in range(1, groups):
        pl.semaphore_signal(barrier, inc=1, device_id=(group_of(t), d), device_id_type=MESH)

    started = []

    def remote(src, dst, send, recv, target):
        return pltpu.make_async_remote_copy(
            src_ref=src, dst_ref=dst, send_sem=send, recv_sem=recv, device_id=target, device_id_type=MESH
        )

    lane_i = lax.broadcasted_iota(jnp.int32, (LANES, LANES), 0)
    lane_j = lax.broadcasted_iota(jnp.int32, (LANES, LANES), 1)
    averaging = jnp.where(lane_i // BAND == lane_j // BAND, 1.0 / BAND, 0.0).astype(bf16)
    tiles = F // LANES

    def whiten():
        for s in range(2):
            for l in range(tiles):
                cols = slice(l * LANES, (l + 1) * LANES)
                re, im = raw[2 * s, :, cols], raw[2 * s + 1, :, cols]
                mag[(s * tiles + l) * channels:(s * tiles + l + 1) * channels, :] = jnp.sqrt(re * re + im * im)
        value = mag[...]
        high = value.astype(bf16)
        rest = value - high.astype(f32)
        mid = rest.astype(bf16)
        low = (rest - mid.astype(f32)).astype(bf16)
        mean = (
            jnp.dot(high, averaging, preferred_element_type=f32)
            + jnp.dot(mid, averaging, preferred_element_type=f32)
            + jnp.dot(low, averaging, preferred_element_type=f32)
        )
        mag[...] = 1.0 / (mean + 1e-05)
        for s in range(2):
            for l in range(tiles):
                cols = slice(l * LANES, (l + 1) * LANES)
                inverse = mag[(s * tiles + l) * channels:(s * tiles + l + 1) * channels, :]
                for p in range(2):
                    scaled = raw[2 * s + p, :, cols] * inverse
                    white[2 * s + p, :, cols] = scaled.astype(bf16).astype(f32)

    def pick_row(channel, to):
        for sp in range(4):
            for i in range(CHUNKS):
                to[sp * CHUNKS + i:sp * CHUNKS + i + 1, :] = white[
                    sp, pl.ds(channel, 1), i * WIDE:(i + 1) * WIDE
                ]

    n_sent = [0]

    def forward(j, target, when=None):
        copy = remote(gathered.at[j], gathered.at[j], send_sem.at[n_sent[0]], recv_sem.at[j], (g, target))
        n_sent[0] += 1
        if when is None:
            copy.start()
        else:
            pl.when(when)(copy.start)
        started.append((when, copy))

    def arrived(j):
        remote(gathered.at[j], gathered.at[j], send_sem.at[0], recv_sem.at[j], (g, flip_k)).wait_recv()

    def transform(bases, zeros):
        used = 2 * HALF * len(bases)
        y[0:used, :] = jnp.dot(x[0:used, :], table[...], preferred_element_type=f32)
        for n, (base, zero) in enumerate(zip(bases, zeros)):
            turn_back(n * 2 * HALF, base, zero)

    def turn_back(row, base, zero):
        for h in range(2):
            p = [jnp.zeros((8, LANES), f32) for _ in range(2)]
            q = [jnp.zeros((8, LANES), f32) for _ in range(2)]
            for b in range(BLK):
                cos, sin = turn[0, b], turn[1, b]
                real = slice(row + b * 16 + h * 8, row + b * 16 + h * 8 + 8)
                imag = slice(row + HALF + b * 16 + h * 8, row + HALF + b * 16 + h * 8 + 8)
                for u in range(2):
                    on_cos = slice(u * LANES, (u + 1) * LANES)
                    on_sin = slice(HALF + u * LANES, HALF + (u + 1) * LANES)
                    p[u] = p[u] + (cos * y[real, on_cos] - sin * y[real, on_sin])
                    q[u] = q[u] + (cos * y[imag, on_sin] + sin * y[imag, on_cos])
            lane = lax.broadcasted_iota(jnp.int32, (8, LANES), 1)
            back = lax.rem(LANES - lane, LANES)
            turned = [jnp.take_along_axis(p[u] + q[u], back, axis=1) for u in range(2)]
            out = [
                jnp.where(lane == 0, turned[0], turned[1]),
                jnp.where(lane == 0, turned[1], turned[0]),
                jnp.where(lane == 0, zero[h] * SCALE, p[0] - q[0]),
                p[1] - q[1],
            ]
            for n in range(4):
                acc[pl.ds(base + h * 8, 8), n * LANES:(n + 1) * LANES] = out[n]

    def cross(first, n):
        for half in range(2):
            src_f32[2 * n + half] = gathered[first + half].astype(f32)
        total = [jnp.zeros((channels, LANES), f32) for _ in range(2)]
        for l in range(tiles):
            i, lanes = l // 8, slice(l % 8 * LANES, (l % 8 + 1) * LANES)
            w = [white[sp, :, l * LANES:(l + 1) * LANES] for sp in range(4)]
            real, imag = [], []
            for half in range(2):
                v = [
                    jnp.broadcast_to(
                        src_f32[2 * n + half, sp * CHUNKS + i:sp * CHUNKS + i + 1, lanes], (channels, LANES)
                    )
                    for sp in range(4)
                ]
                real.append(w[0] * v[0] + w[1] * v[1] + w[2] * v[2] + w[3] * v[3])
                imag.append(w[1] * v[0] - w[0] * v[1] + w[3] * v[2] - w[2] * v[3])
                total[half] = total[half] + real[-1]
            b, cols = l // 2, slice(l % 2 * LANES, (l % 2 + 1) * LANES)
            row = 2 * HALF * n + b * 16
            x[row:row + 16, cols] = jnp.concatenate(real, axis=0).astype(bf16)
            x[HALF + row:HALF + row + 16, cols] = jnp.concatenate(imag, axis=0).astype(bf16)
        return [jnp.sum(t, axis=1, keepdims=True) for t in total]

    def batch(*firsts):
        zeros = [cross(first, n) for n, first in enumerate(firsts)]
        transform([pl.multiple_of(first * channels, 2 * channels) for first in firsts], zeros)

    for copy in loads:
        copy.wait()
    whiten()
    pick_row(pick_ref[0], row_scratch)
    gathered[d] = row_scratch[...].astype(bf16)
    remote_load.wait()
    for t in range(1, groups):
        h = group_of(t)
        for slot in range(slots):
            req_out[t, slot:slot + 1, :] = jnp.full((1, LANES), remote_ref[0, 0, h, slot], jnp.int32)

    pl.semaphore_wait(barrier, rows + 2 + groups - 1 + (r + DIRECT) // rows * c * (g == 0))
    straight = (r >= rows - DIRECT) & (c == 1) & (g == 0)
    forward(d, across[0] % 4, straight)
    for t in range(rows - 1, 0, -1):
        forward(d, row_of(t) * 4 + c * 2 + k)
    for target in [flip_k] + across:
        forward(d, target)
    for t in range(1, groups):
        copy = remote(req_out.at[t], req_in.at[g], req_send.at[t], req_recv.at[g], (group_of(t), d))
        copy.start()
        started.append((None, copy))

    table_load.wait()
    turn_load.wait()
    pairs = (groups - 1) * slots
    local_load.wait()
    pr[...] = jnp.zeros_like(pr)
    pi[...] = jnp.zeros_like(pi)
    for n in range(pairs):
        pick_row(local_ref[0, 0, group_of(n // slots + 1), n % slots], local_rows.at[n])
    arrived(flip_k)
    batch(r * 4 + c * 2)

    channel_id = lax.broadcasted_iota(jnp.int32, (channels, LANES), 0)
    for t in range(1, groups):
        h = group_of(t)
        remote(req_out.at[t], req_in.at[h], req_send.at[t], req_recv.at[h], (h, d)).wait_recv()
        asked = req_in[h]
        for slot in range(slots):
            chosen = channel_id == jnp.broadcast_to(asked[slot:slot + 1, :], (channels, LANES))
            chosen = jnp.concatenate([chosen] * (WIDE // LANES), axis=1)
            for sp in range(4):
                for q in range(CHUNKS):
                    part = jnp.where(chosen, white[sp, :, q * WIDE:(q + 1) * WIDE], 0.0)
                    row_scratch[sp * CHUNKS + q:sp * CHUNKS + q + 1, :] = jnp.sum(part, axis=0, keepdims=True)
            rows_out[t, slot * 16:(slot + 1) * 16, :] = row_scratch[...].astype(bf16)
        copy = remote(rows_out.at[t], rows_in.at[g], row_send.at[t], row_recv.at[g], (h, d))
        copy.start()
        started.append((None, copy))

    for t in range(1, rows):
        j = row_of(t) * 4 + c * 2 + k
        arrived(j)
        for target in across:
            forward(j, target, (r > 0) | (c == 0) | (g > 0) if t >= rows - DIRECT else None)
        forward(j, flip_k)

    def near(t):
        first = row_of(t) * 4 + c * 2
        arrived(first + (1 - k))
        return first

    def far(t):
        first = row_of(t) * 4 + (1 - c) * 2
        arrived(first + (1 - k))
        pl.when(jnp.logical_or(r + c + g > 0, row_of(t) < rows - DIRECT))(functools.partial(arrived, first + k))
        return first

    def in_twos(wait, first_t, end_t):
        if (end_t - first_t) % 2:
            batch(wait(first_t))
            first_t += 1
        for t in range(first_t, end_t, 2):
            batch(wait(t), wait(t + 1))

    batch(far(0), near(1))
    for row in range(rows - DIRECT, rows):
        j = row * 4 + across[0] % 4
        pl.when(r + c + g == 0)(functools.partial(arrived, j))
        forward(j, flip_k, r + c + g == 0)

    in_twos(near, 2, rows)

    count_load.wait()
    cross_out[0, 0, g] = jnp.zeros((slots, LAGS), f32)
    for base in range(0, pairs, 16):
        for n in range(base, min(base + 16, pairs)):
            t, slot = n // slots + 1, n % slots
            h = group_of(t)
            if slot == 0:
                remote(rows_out.at[t], rows_in.at[h], row_send.at[t], row_recv.at[h], (h, d)).wait_recv()
            there = rows_in[h, slot * 16:(slot + 1) * 16, :].astype(f32)
            here = local_rows[n]
            w = [here[sp * CHUNKS:(sp + 1) * CHUNKS] for sp in range(4)]
            v = [there[sp * CHUNKS:(sp + 1) * CHUNKS] for sp in range(4)]
            real = w[0] * v[0] + w[1] * v[1] + w[2] * v[2] + w[3] * v[3]
            imag = w[1] * v[0] - w[0] * v[1] + w[3] * v[2] - w[2] * v[3]
            for q in range(CHUNKS):
                pr[n - base:n - base + 1, q * WIDE:(q + 1) * WIDE] = real[q:q + 1]
                pi[n - base:n - base + 1, q * WIDE:(q + 1) * WIDE] = imag[q:q + 1]
        for b in range(BLK):
            x[b * 16:(b + 1) * 16, :] = pr[:, b * INNER:(b + 1) * INNER].astype(bf16)
            x[HALF + b * 16:HALF + (b + 1) * 16, :] = pi[:, b * INNER:(b + 1) * INNER].astype(bf16)
        zero = [jnp.sum(pr[h * 8:(h + 1) * 8, :], axis=1, keepdims=True) for h in range(2)]
        transform([n_dev * channels], [zero])
        for n in range(base, min(base + 16, pairs)):
            t, slot = n // slots + 1, n % slots
            h = group_of(t)
            row = n_dev * channels + n - base
            keep = jnp.where(slot < count_ref[0, 0, h], 1.0, 0.0)
            cross_out[0, 0, h, slot:slot + 1, :] = acc[row:row + 1, :] * keep

    in_twos(far, 1, rows - 1)
    batch(far(rows - 1))

    for when, copy in started:
        if when is None:
            copy.wait_send()
        else:
            pl.when(when)(copy.wait_send)


def store(n_dev, acc, cross_in, group_out, cross_out, sem):
    channels = group_out.shape[0]
    copies = [
        pltpu.make_async_copy(acc.at[0:n_dev, ch, :], group_out.at[ch], sem.at[ch]) for ch in range(channels)
    ] + [pltpu.make_async_copy(cross_in, cross_out, sem.at[channels])]
    for copy in copies:
        copy.start()
    for copy in copies:
        copy.wait()


def solution(mesh):
    groups, n_dev = mesh.shape["grp"], mesh.shape["dev"]
    table, turn = lag_tables()

    def on_device(spectra, source_pick, pair_remote, pair_local, pair_count):
        channels = spectra.shape[0]
        slots = pair_remote.shape[3]
        total = n_dev * channels + 16
        hbm = pl.BlockSpec(memory_space=pltpu.HBM)
        vmem = pl.BlockSpec(memory_space=pltpu.VMEM)
        anywhere = pl.BlockSpec(memory_space=pl.ANY)
        held = [
            pltpu.with_memory_space_constraint(a, pltpu.HBM)
            for a in (pair_remote, pair_local, pair_count, spectra, jnp.asarray(table), jnp.asarray(turn))
        ]
        cross_shape = (1, 1, groups, slots, LAGS)
        sends = DIRECT + 2 + 3 * rows_of(n_dev) + rows_of(n_dev) - 1
        acc, cross = pl.pallas_call(
            functools.partial(kernel, groups, n_dev, slots, channels),
            out_shape=(pltpu.VMEM((total, LAGS), f32), pltpu.VMEM(cross_shape, f32)),
            in_specs=[pl.BlockSpec(memory_space=pltpu.SMEM)] + [hbm] * 6,
            out_specs=(vmem, vmem),
            scratch_shapes=[
                pltpu.VMEM((4, channels, F), f32),
                pltpu.VMEM((4, channels, F), f32),
                pltpu.VMEM((2 * F // LANES * channels, LANES), f32),
                pltpu.VMEM((n_dev, 16, WIDE), bf16),
                pltpu.VMEM((16, WIDE), f32),
                pltpu.VMEM((4, 16, WIDE), f32),
                pltpu.VMEM((4 * HALF, INNER), bf16),
                pltpu.VMEM((4 * HALF, 2 * HALF), f32),
                pltpu.VMEM(table.shape, bf16),
                pltpu.VMEM(turn.shape, f32),
                pltpu.VMEM((16, F), f32),
                pltpu.VMEM((16, F), f32),
                pltpu.VMEM(((groups - 1) * slots, 16, WIDE), f32),
                pltpu.VMEM((groups, 8, LANES), jnp.int32),
                pltpu.VMEM((groups, 8, LANES), jnp.int32),
                pltpu.VMEM((groups, slots * 16, WIDE), bf16),
                pltpu.VMEM((groups, slots * 16, WIDE), bf16),
                pltpu.SMEM(pair_remote.shape, jnp.int32),
                pltpu.SMEM(pair_local.shape, jnp.int32),
                pltpu.SMEM(pair_count.shape, jnp.int32),
                pltpu.SemaphoreType.DMA((4,)),
                pltpu.SemaphoreType.DMA((5,)),
                pltpu.SemaphoreType.DMA((sends,)),
                pltpu.SemaphoreType.DMA((n_dev,)),
                pltpu.SemaphoreType.DMA((groups,)),
                pltpu.SemaphoreType.DMA((groups,)),
                pltpu.SemaphoreType.DMA((groups,)),
                pltpu.SemaphoreType.DMA((groups,)),
            ],
            compiler_params=pltpu.CompilerParams(
                collective_id=0, has_side_effects=True, vmem_limit_bytes=48 << 20
            ),
        )(source_pick, *held)
        return pl.pallas_call(
            functools.partial(store, n_dev),
            out_shape=(
                jax.ShapeDtypeStruct((channels, n_dev, LAGS), f32),
                jax.ShapeDtypeStruct(cross_shape, f32),
            ),
            in_specs=[anywhere, anywhere],
            out_specs=(anywhere, anywhere),
            scratch_shapes=[pltpu.SemaphoreType.DMA((channels + 1,))],
            compiler_params=pltpu.CompilerParams(vmem_limit_bytes=1 << 20),
        )(acc.reshape(total // channels, channels, LAGS), cross)

    return jax.shard_map(
        on_device,
        mesh=mesh,
        in_specs=(
            P(("grp", "dev"), None, None, None),
            P(("grp", "dev")),
            P("grp", "dev", None, None),
            P("grp", "dev", None, None),
            P("grp", "dev", None),
        ),
        out_specs=(P(("grp", "dev"), None, None), P("grp", "dev", None, None, None)),
        check_vma=False,
    )


def rows_of(n_dev):
    return n_dev // 4
```
